32 devices in a mesh: lat: 8 (over y, x, core), lon: 4 (over z).
Axes of the slice: x: 2, y: 2, z: 4, core: 2. Of those that a mesh axis runs over, the one named last changes fastest.
Arguments:
- level_fields: float32 [2, 2, 640, 2560], P(None, None, 'lat', 'lon'), may hold values from -6 to 6
- wind_field: float32 [2, 2, 640, 2560], P(None, None, 'lat', 'lon'), may hold values from -6 to 6
- zonal_step: float32 [640], P('lat'), may hold values from 0.1 to 1
- quad_weight: float32 [640], P('lat'), may hold values from 0.005 to 0.05
- legendre: bfloat16 [640, 640, 640], P('lon', 'lat'), may hold values from -6 to 6
- wave_table: int32 [640], replicated, may hold values from 0 to 639, as said below
- damping: float32 [2], replicated, may hold values from 0.5 to 20
- vertical: float32 [2, 2], replicated, may hold values from -4 to 4
Outputs:
- new_fields: float32 [2, 2, 640, 2560], P(None, None, 'lat', 'lon')
- spectrum: float32 [640, 640, 2, 2], P('lat', 'lon')
The draws below stay inside these ranges and needn't reach their ends.
Inputs may be any that keep to these rules, and one draw needn't show every extreme that they name: `wave_table`: slots 2k and 2k+1 hold wavenumbers p and 639 - p; every wavenumber appears in exactly one slot.
All inputs are finite; a program needn't handle non-finite values.
Results may differ from the reference program's by a relative error of at most 0.0038.
Values may be sent and summed in bfloat16 or wider, within the bound.
No kernel may reach another device: no remote copies, remote signals or barrier semaphores. Data moves between devices by JAX's collectives and lax.ppermute only.
A program may use at most 64 MiB of HBM per device.

```python
import math
import jax
import jax.numpy as jnp
from jax import lax

NLON = 2560
M = 640
LEVELS = 2
NHALF = 640


def draw_wave_table(key, part):
    order = jax.random.permutation(key, M // 2).astype(jnp.int32)
    return jnp.stack([order, M - 1 - order], axis=1).reshape(M)


def shard_levels(rng, extent, cuts, smallest, top_value):
    def one(dim, blocks):
        draws = jax.random.uniform(jax.random.fold_in(jax.random.fold_in(rng, 6), dim), (blocks,), jnp.float32, smallest / len(cuts), top_value / len(cuts))
        return jnp.repeat(jnp.exp(draws), extent[dim] // blocks).reshape((-1,) + (1,) * (len(extent) - dim - 1))

    loudness = one(*cuts[0])
    for cut in cuts[1:]:
        loudness = loudness * one(*cut)
    return loudness


def centred(key, dims, spread, limit, pieces=(), kind=jnp.bfloat16):
    level = shard_levels(key, dims, pieces, -0.22, 0.18) if pieces else 1.0
    entries = jax.random.normal(key, dims, jnp.float32) * spread * level
    return jnp.minimum(jnp.maximum(entries, -limit), limit).astype(kind)


def setup_inputs(seed: int = 0) -> dict:
    keys = jax.random.split(jax.random.key(seed), 9)
    return {
        "level_fields": centred(keys[0], (LEVELS, 2, NHALF, NLON), 1.0, 6.0, ((2, 8), (3, 4)), jnp.float32),
        "wind_field": centred(keys[1], (2, 2, NHALF, NLON), 1.0, 6.0, ((2, 8), (3, 4)), jnp.float32),
        "zonal_step": jnp.clip(jnp.exp(math.log(1.0) - 2.3025851 * jax.random.uniform(keys[2], (NHALF,), jnp.float32) ** shard_levels(keys[2], (NHALF,), ((0, 8),), -0.2, 0.2)), 0.1, 1.0),
        "quad_weight": jnp.clip(jnp.exp(math.log(0.05) - 2.3025851 * jax.random.uniform(keys[3], (NHALF,), jnp.float32) ** shard_levels(keys[3], (NHALF,), ((0, 8),), -0.2, 0.2)), 0.005, 0.05),
        "legendre": centred(keys[4], (M, NHALF, M), 1.0, 6.0, ((0, 4), (1, 8))),
        "wave_table": draw_wave_table(jax.random.fold_in(keys[8], 71), 0),
        "damping": jnp.clip(jnp.exp(jax.random.uniform(keys[6], (LEVELS,), jnp.float32, math.log(0.5), math.log(20.0))), 0.5, 20.0),
        "vertical": centred(keys[7], (LEVELS, LEVELS), LEVELS ** -0.5, 4.0, (), jnp.float32),
    }


HIGHEST_PRECISION = lax.Precision.HIGHEST

def angle_table(waves, columns):
    return (waves[:, None] * columns[None, :] % NLON).astype(jnp.float32) * (2.0 * math.pi / NLON)

def advect(level_fields, wind_field, zonal_step):
    eastward = jnp.roll(level_fields, -1, axis=3)
    westward = jnp.roll(level_fields, 1, axis=3)
    equator_row = level_fields[:, ::-1, -1:, :]
    toward = jnp.concatenate([level_fields[:, :, 1:, :], equator_row], axis=2)
    poleward = jnp.concatenate([jnp.zeros_like(level_fields[:, :, :1, :]), level_fields[:, :, :-1, :]], axis=2)
    tendency = wind_field[0] * zonal_step[:, None] * (eastward - westward) + 0.25 * wind_field[1] * (toward - poleward)
    return level_fields - tendency

def correct(spectrum, degrees, damping, vertical):
    modal = jnp.einsum('kl,nmcl->nmck', vertical, spectrum, precision=HIGHEST_PRECISION)
    divisor = 1.0 + damping[None, :] * (degrees * (degrees + 1)).astype(jnp.float32)[:, None] / float(M * M)
    modal = modal / divisor[:, None, None, :]
    return jnp.einsum('kl,nmck->nmcl', vertical, modal, precision=HIGHEST_PRECISION)

def reference(level_fields, wind_field, zonal_step, quad_weight, legendre, wave_table, damping, vertical):
    stepped = advect(level_fields, wind_field, zonal_step)
    flat_grid = stepped.reshape(-1, NLON)
    angles = angle_table(wave_table, jnp.arange(NLON, dtype=jnp.int32))
    cosine_part = jnp.dot(jnp.cos(angles), flat_grid.T, precision=HIGHEST_PRECISION)
    sine_part = -jnp.dot(jnp.sin(angles), flat_grid.T, precision=HIGHEST_PRECISION)
    fourier = jnp.stack([cosine_part, sine_part], axis=1) / math.sqrt(NLON)
    weighted = (fourier.reshape(M, 2, LEVELS, 2, NHALF) * quad_weight).astype(jnp.bfloat16)
    weighted = weighted.reshape(M, 4 * LEVELS, NHALF)
    degrees = jnp.arange(M, dtype=jnp.int32)

    def forward_slot(inputs):
        weight_slot, table_slot, wave = inputs
        summed = jnp.dot(weight_slot, table_slot, preferred_element_type=jnp.float32).reshape(2, LEVELS, 2, M)
        parity = jnp.where((degrees - wave) % 2 == 0, 1.0, -1.0)
        combined = summed[:, :, 0] + parity * summed[:, :, 1]
        return jnp.where(degrees >= wave, combined, 0.0)
    raw = lax.map(forward_slot, (weighted, legendre, wave_table))
    raw = raw.transpose(3, 0, 1, 2)
    spectrum = correct(raw, degrees, damping, vertical)
    rounded = spectrum.astype(jnp.bfloat16).transpose(1, 0, 2, 3).reshape(M, M, 2 * LEVELS)

    def inverse_slot(inputs):
        table_slot, coef_slot, wave = inputs
        even_mask = ((degrees - wave) % 2 == 0)[:, None]
        even_part = jnp.dot(table_slot, jnp.where(even_mask, coef_slot, 0), preferred_element_type=jnp.float32)
        odd_part = jnp.dot(table_slot, jnp.where(even_mask, 0, coef_slot), preferred_element_type=jnp.float32)
        return jnp.stack([even_part + odd_part, even_part - odd_part], axis=0) / math.sqrt(M)
    coefs = lax.map(inverse_slot, (legendre, rounded, wave_table))
    coefs = coefs.reshape(M, 2, NHALF, 2, LEVELS).transpose(0, 3, 4, 1, 2).reshape(M, 2, -1)
    factor = jnp.where(wave_table == 0, 1.0, 2.0)[:, None]
    grid_out = jnp.dot(coefs[:, 0].T, jnp.cos(angles) * factor, precision=HIGHEST_PRECISION)
    grid_out = grid_out - jnp.dot(coefs[:, 1].T, jnp.sin(angles) * factor, precision=HIGHEST_PRECISION)
    new_fields = (grid_out / math.sqrt(NLON)).reshape(LEVELS, 2, NHALF, NLON)
    return (new_fields, spectrum)
```

```python
import math

import jax
import jax.numpy as jnp
from jax import lax
from jax.experimental import pallas as pl
from jax.experimental.pallas import tpu as pltpu
from jax.sharding import PartitionSpec as P

NLON = 2560
M = 640


HIGHEST_PRECISION = lax.Precision.HIGHEST


def padded(cells, sides, width):
    for axis, dim in sides:
        count = lax.axis_size(axis)
        head = lax.slice_in_dim(cells, 0, width, axis=dim)
        tail = lax.slice_in_dim(cells, cells.shape[dim] - width, cells.shape[dim], axis=dim)
        cells = jnp.concatenate(
            [
                lax.ppermute(tail, axis, [(i, (i + 1) % count) for i in range(count)]),
                cells,
                lax.ppermute(head, axis, [((i + 1) % count, i) for i in range(count)]),
            ],
            axis=dim,
        )
    return cells


def angle_table(waves, columns):
    return (waves[:, None] * columns[None, :] % NLON).astype(jnp.float32) * (2.0 * math.pi / NLON)


def correct(spectrum, degrees, damping, vertical):
    modal = jnp.einsum("kl,nmcl->nmck", vertical, spectrum, precision=HIGHEST_PRECISION)
    divisor = 1.0 + damping[None, :] * (degrees * (degrees + 1)).astype(jnp.float32)[
        :, None
    ] / float(M * M)
    modal = modal / divisor[:, None, None, :]
    return jnp.einsum("kl,nmck->nmcl", vertical, modal, precision=HIGHEST_PRECISION)


def untiled(
    level_fields, wind_field, zonal_step, quad_weight, legendre, wave_table, damping, vertical
):
    levels, hemis, rows_half, lon_dev = level_fields.shape
    slots_dev = legendre.shape[0]
    lat_count = lax.axis_size("lat")
    lat_index = lax.axis_index("lat")
    lon_index = lax.axis_index("lon")
    degree_dev = M // lat_count
    grid_count = levels * hemis * rows_half
    contract_last = (((1,), (1,)), ((), ()))
    contract_first = (((0,), (0,)), ((), ()))
    batch_slots = (((2,), (1,)), ((0,), (0,)))
    extended = padded(level_fields, (("lat", 2), ("lon", 3)), 1)
    eastward = extended[:, :, 1:-1, 2:]
    westward = extended[:, :, 1:-1, :-2]
    toward = extended[:, :, 2:, 1:-1]
    poleward = extended[:, :, :-2, 1:-1]
    row_number = jnp.arange(rows_half)
    at_equator = (row_number == rows_half - 1) & (lat_index == lat_count - 1)
    toward = jnp.where(at_equator[:, None], level_fields[:, ::-1, -1:, :], toward)
    at_pole = (row_number == 0) & (lat_index == 0)
    poleward = jnp.where(at_pole[:, None], 0.0, poleward)
    tendency = wind_field[0] * zonal_step[:, None] * (eastward - westward) + 0.25 * wind_field[
        1
    ] * (toward - poleward)
    stepped = level_fields - tendency
    my_waves = lax.dynamic_slice_in_dim(wave_table, lon_index * slots_dev, slots_dev)
    portion = lax.all_gather(stepped, "lon", axis=3, tiled=True)
    lon_width = portion.shape[3]
    columns = jnp.arange(lon_width, dtype=jnp.int32)
    angles = angle_table(my_waves, columns)
    values = portion.reshape(grid_count, lon_width)
    cosine_sum = lax.dot_general(
        jnp.cos(angles), values, contract_last, precision=HIGHEST_PRECISION
    )
    sine_sum = lax.dot_general(jnp.sin(angles), values, contract_last, precision=HIGHEST_PRECISION)
    cosine_sum, sine_sum = (cosine_sum, sine_sum)
    fourier = jnp.stack([cosine_sum, -sine_sum], axis=1) / math.sqrt(NLON)
    weighted = (fourier.reshape(slots_dev, 2, levels, hemis, rows_half) * quad_weight).astype(
        jnp.bfloat16
    )
    weighted = weighted.reshape(slots_dev, 2 * levels * hemis, rows_half)
    table_part = legendre
    summed = lax.dot_general(weighted, table_part, batch_slots, preferred_element_type=jnp.float32)
    summed = summed.reshape(slots_dev, 2, levels, hemis, degree_dev * lax.axis_size("lat"))
    degrees = jnp.arange(degree_dev * lax.axis_size("lat"), dtype=jnp.int32)
    parity = jnp.where((degrees[None, :] - my_waves[:, None]) % 2 == 0, 1.0, -1.0)
    kept_mask = degrees[None, :] >= my_waves[:, None]
    combined = summed[:, :, :, 0] + parity[:, None, None, :] * summed[:, :, :, 1]
    combined = jnp.where(kept_mask[:, None, None, :], combined, 0.0)
    raw = lax.psum_scatter(combined.transpose(3, 0, 1, 2), "lat", scatter_dimension=0, tiled=True)
    my_degrees = lat_index * degree_dev + jnp.arange(degree_dev, dtype=jnp.int32)
    spectrum = correct(raw, my_degrees, damping, vertical)
    portion = lax.all_gather(spectrum.astype(jnp.bfloat16), "lat", axis=0, tiled=True)
    row_count = portion.shape[0]
    table_part = legendre
    degrees = jnp.arange(row_count, dtype=jnp.int32)
    even_mask = ((degrees[None, :] - my_waves[:, None]) % 2 == 0)[:, :, None]
    arranged = portion.transpose(1, 0, 2, 3).reshape(slots_dev, row_count, 2 * levels)
    even_sum = lax.dot_general(
        table_part,
        jnp.where(even_mask, arranged, 0),
        batch_slots,
        preferred_element_type=jnp.float32,
    )
    odd_sum = lax.dot_general(
        table_part,
        jnp.where(even_mask, 0, arranged),
        batch_slots,
        preferred_element_type=jnp.float32,
    )
    even_sum, odd_sum = (even_sum, odd_sum)
    coefs = jnp.stack([even_sum + odd_sum, even_sum - odd_sum], axis=1) / math.sqrt(M)
    coefs = (
        coefs.reshape(slots_dev, 2, rows_half, 2, levels)
        .transpose(0, 3, 4, 1, 2)
        .reshape(slots_dev, 2, grid_count)
    )
    my_columns = lon_index * lon_dev + jnp.arange(lon_dev, dtype=jnp.int32)
    portion = lax.all_gather(coefs, "lon", axis=0, tiled=True)
    factor = jnp.where(wave_table == 0, 1.0, 2.0)[:, None]
    angles = angle_table(wave_table, my_columns)
    totals = lax.dot_general(
        portion[:, 0], jnp.cos(angles) * factor, contract_first, precision=HIGHEST_PRECISION
    )
    grid_out = totals - lax.dot_general(
        portion[:, 1], jnp.sin(angles) * factor, contract_first, precision=HIGHEST_PRECISION
    )
    new_fields = (grid_out / math.sqrt(NLON)).reshape(level_fields.shape)
    return (new_fields, spectrum)


CHUNKS = 2
GROUP = 16
F32 = jnp.float32
BF16 = jnp.bfloat16


def split_halves(value):
    high = value.astype(BF16)
    return high, (value - high.astype(F32)).astype(BF16)


def dot_rows(left, right):
    return lax.dot_general(left, right, (((1,), (1,)), ((), ())), preferred_element_type=F32)


def dot_columns(left, right):
    return lax.dot_general(left, right, (((0,), (0,)), ((), ())), preferred_element_type=F32)


def partner_pairs(count, step):
    return [(i, i ^ step) for i in range(count)]


def zonal_sums_kernel(blocks, share, first, grid_ref, cosine_ref, sine_ref, *outs):
    high, low = split_halves(grid_ref[...])
    count = grid_ref.shape[0]
    per_block = cosine_ref.shape[0] // blocks
    for part, table in enumerate((cosine_ref, sine_ref)):
        rows = jnp.concatenate(
            [table[k * per_block + first : k * per_block + first + share, :] for k in range(blocks)],
            axis=0,
        )
        rows_high, rows_low = split_halves(rows)
        sums = dot_rows(rows_high, high) + (dot_rows(rows_high, low) + dot_rows(rows_low, high))
        for k, out in enumerate(outs):
            out[:, part * count : (part + 1) * count] = sums[
                k * share : (k + 1) * share, :
            ].astype(out.dtype)


def forward_kernel(
    parts, sections, rows, degree_dev, lat_count, waves_ref, place_ref, *refs
):
    received = refs[:parts]
    weight_ref, table_ref = refs[parts : parts + 2]
    outs = refs[parts + 2 : parts + 2 + lat_count]
    spread_ref, kept_ref, turned_ref = refs[parts + 2 + lat_count :]
    step = pl.program_id(0)
    half = sections // 2
    levels = half // 2
    group = table_ref.shape[0]
    columns = table_ref.shape[2]

    @pl.when(step == 0)
    def _():
        total = received[0][...].astype(F32)
        for other in received[1:]:
            total = total + other[...].astype(F32)
        total = total * weight_ref[...]
        for c in range(2):
            for level in range(levels):
                for h in range(2):
                    at = ((c * levels + level) * 2 + h) * rows
                    spread_ref[:, h * half + c * levels + level, 0:rows] = total[:, at : at + rows]

    degree = lax.broadcasted_iota(jnp.int32, (1, columns), 1)
    for u in range(group):
        slot = step * group + u
        wave = waves_ref[slot]
        high, low = split_halves(spread_ref[slot, :, 0:rows])
        both = jnp.concatenate([high.astype(F32), low.astype(F32)], axis=0).astype(BF16)
        sums = jnp.dot(both, table_ref[u], preferred_element_type=F32)
        sums = sums[:sections] + sums[sections:]
        sign = jnp.where((degree - wave) & 1 == 0, 1.0, -1.0)
        combined = jnp.where(degree >= wave, sums[:half] + sign * sums[half:], 0.0)
        kept_ref[:, slot, :] = combined

    @pl.when(step == pl.num_programs(0) - 1)
    def _():
        for j in range(half):
            turned_ref[j] = kept_ref[j].T
        for k, out in enumerate(outs):
            start = pl.multiple_of((place_ref[0] ^ k) * degree_dev, 8)
            out[...] = turned_ref[:, pl.ds(start, degree_dev), :].astype(out.dtype)


def inverse_kernel(parts, sections, rows, degree_dev, waves_ref, place_ref, *refs):
    received = refs[:parts]
    table_ref, out_ref, joined_ref, kept_ref, spread_ref = refs[parts:]
    step = pl.program_id(0)
    half = sections // 2
    levels = half // 2
    group = table_ref.shape[0]
    columns = table_ref.shape[2]

    @pl.when(step == 0)
    def _():
        for k, part in enumerate(received):
            start = pl.multiple_of((place_ref[0] ^ k) * degree_dev, 8)
            joined_ref[:, pl.ds(start, degree_dev), :] = part[...].astype(F32)
        for j in range(half):
            kept_ref[j] = joined_ref[j].T

    degree = lax.broadcasted_iota(jnp.int32, (1, columns), 1)
    for u in range(group):
        slot = step * group + u
        wave = waves_ref[slot]
        values = kept_ref[:, slot, :]
        even = (degree - wave) & 1 == 0
        both = jnp.concatenate(
            [jnp.where(even, values, 0.0), jnp.where(even, 0.0, values)], axis=0
        ).astype(BF16)
        sums = dot_rows(both, table_ref[u])
        factor = jnp.where(wave == 0, 1.0, 2.0) / math.sqrt(M)
        sums = sums * factor
        spread_ref[slot, 0:half, 0:rows] = sums[:half] + sums[half:]
        spread_ref[slot, half:sections, 0:rows] = sums[:half] - sums[half:]

    @pl.when(step == pl.num_programs(0) - 1)
    def _():
        for c in range(2):
            for level in range(levels):
                for h in range(2):
                    at = ((c * levels + level) * 2 + h) * rows
                    out_ref[:, at : at + rows] = spread_ref[
                        :, h * half + c * levels + level, 0:rows
                    ].astype(out_ref.dtype)


def zonal_values_kernel(blocks, share, first, cosine_ref, sine_ref, base_ref, *refs):
    received, out = refs[:-1], refs[-1]
    count = out.shape[0]
    per_block = cosine_ref.shape[0] // blocks
    total = base_ref[...] if base_ref.shape == out.shape else None
    for part, table in enumerate((cosine_ref, sine_ref)):
        rows = jnp.concatenate(
            [table[k * per_block + first : k * per_block + first + share, :] for k in range(blocks)],
            axis=0,
        )
        coefs = jnp.concatenate(
            [other[:, part * count : (part + 1) * count] for other in received], axis=0
        )
        rows_high, rows_low = split_halves(rows)
        term = dot_columns(coefs, rows_high) + dot_columns(coefs, rows_low)
        total = term if total is None else total + term
    out[...] = total


VMEM = pl.BlockSpec(memory_space=pltpu.VMEM)


def limits(size):
    return pltpu.CompilerParams(vmem_limit_bytes=size << 20)


def shards(
    level_fields, wind_field, zonal_step, quad_weight, legendre, wave_table, damping, vertical
):
    levels, hemis, rows_half, lon_dev = level_fields.shape
    slots_dev, _, columns = legendre.shape
    lat_count = lax.axis_size("lat")
    lon_count = lax.axis_size("lon")
    degree_dev = columns // lat_count
    share = slots_dev // CHUNKS
    if (
        rows_half % 16
        or degree_dev % 16
        or lon_dev % 128
        or slots_dev % (CHUNKS * GROUP)
        or levels * hemis != 4
        or lat_count & (lat_count - 1)
        or lon_count & (lon_count - 1)
    ):
        return untiled(
            level_fields,
            wind_field,
            zonal_step,
            quad_weight,
            legendre,
            wave_table,
            damping,
            vertical,
        )
    lat_index = lax.axis_index("lat")
    lon_index = lax.axis_index("lon")
    grid_count = levels * hemis * rows_half
    sections = 2 * levels * hemis
    half = sections // 2
    width = 2 * grid_count

    up = [(i, (i + 1) % lat_count) for i in range(lat_count)]
    east = [(i, (i + 1) % lon_count) for i in range(lon_count)]
    down = [(j, i) for i, j in up]
    west = [(j, i) for i, j in east]
    above = lax.ppermute(level_fields[:, :, -1, :], "lat", up)
    below = lax.ppermute(level_fields[:, :, 0, :], "lat", down)
    before = lax.ppermute(level_fields[:, :, :, -1], "lon", east)
    after = lax.ppermute(level_fields[:, :, :, 0], "lon", west)

    order = [
        lax.dynamic_slice_in_dim(
            wave_table, (lon_index ^ k) * slots_dev, slots_dev
        )
        for k in range(lon_count)
    ]
    my_waves = order[0]
    waves = jnp.concatenate(order)
    piece = 128
    near = angle_table(waves, jnp.arange(piece, dtype=jnp.int32))
    far = angle_table(
        waves, lon_index * lon_dev + piece * jnp.arange(lon_dev // piece, dtype=jnp.int32)
    )
    near_cos, near_sin = jnp.cos(near), jnp.sin(near)
    far_cos, far_sin = jnp.cos(far) / math.sqrt(NLON), jnp.sin(far) / math.sqrt(NLON)
    cosine = jnp.concatenate(
        [
            far_cos[:, j : j + 1] * near_cos - far_sin[:, j : j + 1] * near_sin
            for j in range(lon_dev // piece)
        ],
        axis=1,
    )
    sine = jnp.concatenate(
        [
            -far_sin[:, j : j + 1] * near_cos - far_cos[:, j : j + 1] * near_sin
            for j in range(lon_dev // piece)
        ],
        axis=1,
    )

    above = jnp.where(lat_index == 0, 0.0, above)
    below = jnp.where(lat_index == lat_count - 1, level_fields[:, ::-1, -1, :], below)
    eastward = jnp.concatenate([level_fields[..., 1:], after[..., None]], axis=3)
    westward = jnp.concatenate([before[..., None], level_fields[..., :-1]], axis=3)
    toward = jnp.concatenate([level_fields[:, :, 1:], below[:, :, None]], axis=2)
    poleward = jnp.concatenate([above[:, :, None], level_fields[:, :, :-1]], axis=2)
    tendency = wind_field[0] * zonal_step[:, None] * (eastward - westward) + 0.25 * wind_field[
        1
    ] * (toward - poleward)
    stepped = (level_fields - tendency).reshape(grid_count, lon_dev)

    place = lat_index.astype(jnp.int32).reshape(1)
    weight_row = jnp.tile(quad_weight, sections)[None, :]
    degrees = (lat_index * degree_dev + jnp.arange(degree_dev, dtype=jnp.int32))[:, None]
    growth = (degrees * (degrees + 1)).astype(F32) / float(M * M)
    table_spec = lambda chunk: pl.BlockSpec(
        (GROUP, rows_half, columns), lambda g, *_: (chunk * (share // GROUP) + g, 0, 0)
    )
    steps = share // GROUP

    def zonal_sums(chunk):
        return pl.pallas_call(
            lambda *refs: zonal_sums_kernel(lon_count, share, chunk * share, *refs),
            out_shape=[
                jax.ShapeDtypeStruct((share, width), BF16 if k else F32) for k in range(lon_count)
            ],
            in_specs=[VMEM] * 3,
            out_specs=[VMEM] * lon_count,
            compiler_params=limits(24),
            name=f"zonal_sums_{chunk}",
        )(stepped, cosine, sine)

    def swap_lon(pieces):
        return [pieces[0]] + [
            lax.ppermute(pieces[k], "lon", partner_pairs(lon_count, k))
            for k in range(1, lon_count)
        ]

    def forward(chunk, pieces):
        whole = lambda shape: pl.BlockSpec(shape, lambda *_: (0,) * len(shape))
        return pl.pallas_call(
            lambda *refs: forward_kernel(
                lon_count, sections, rows_half, degree_dev, lat_count, *refs
            ),
            out_shape=[
                jax.ShapeDtypeStruct((half, degree_dev, share), BF16 if k else F32)
                for k in range(lat_count)
            ],
            grid_spec=pltpu.PrefetchScalarGridSpec(
                num_scalar_prefetch=2,
                grid=(steps,),
                in_specs=[whole((share, width))] * lon_count
                + [whole((1, width)), table_spec(chunk)],
                out_specs=[whole((half, degree_dev, share))] * lat_count,
                scratch_shapes=[
                    pltpu.VMEM((share, sections, 128), F32),
                    pltpu.VMEM((half, share, columns), F32),
                    pltpu.VMEM((half, columns, share), F32),
                ],
            ),
            compiler_params=limits(24),
            name=f"forward_{chunk}",
        )(my_waves[chunk * share : (chunk + 1) * share], place, *pieces, weight_row, legendre)

    def correct_chunk(pieces):
        total = pieces[0]
        for k in range(1, lat_count):
            total = total + lax.ppermute(pieces[k], "lat", partner_pairs(lat_count, k)).astype(F32)
        raw = total.reshape(2, levels, degree_dev, share)
        modal = [
            sum(vertical[k, l] * raw[:, l] for l in range(levels)) / (1.0 + damping[k] * growth)
            for k in range(levels)
        ]
        return jnp.stack(
            [sum(vertical[k, l] * modal[k] for k in range(levels)) for l in range(levels)], axis=1
        )

    def inverse(chunk, pieces):
        whole = lambda shape: pl.BlockSpec(shape, lambda *_: (0,) * len(shape))
        return pl.pallas_call(
            lambda *refs: inverse_kernel(lat_count, sections, rows_half, degree_dev, *refs),
            out_shape=jax.ShapeDtypeStruct((share, width), BF16),
            grid_spec=pltpu.PrefetchScalarGridSpec(
                num_scalar_prefetch=2,
                grid=(steps,),
                in_specs=[whole((half, degree_dev, share))] * lat_count + [table_spec(chunk)],
                out_specs=whole((share, width)),
                scratch_shapes=[
                    pltpu.VMEM((half, columns, share), F32),
                    pltpu.VMEM((half, share, columns), F32),
                    pltpu.VMEM((share, sections, 128), F32),
                ],
            ),
            compiler_params=limits(24),
            name=f"inverse_{chunk}",
        )(my_waves[chunk * share : (chunk + 1) * share], place, *pieces, legendre)

    def zonal_values(chunk, pieces, base):
        return pl.pallas_call(
            lambda *refs: zonal_values_kernel(lon_count, share, chunk * share, *refs),
            out_shape=jax.ShapeDtypeStruct((grid_count, lon_dev), F32),
            in_specs=[VMEM] * (3 + lon_count),
            out_specs=VMEM,
            compiler_params=limits(24),
            name=f"zonal_values_{chunk}",
        )(cosine, sine, base, *pieces)

    spectra = []
    coefs = []
    pieces = [swap_lon(zonal_sums(chunk)) for chunk in range(CHUNKS)]
    for chunk in range(CHUNKS):
        spectrum = correct_chunk(forward(chunk, pieces[chunk]))
        spectra.append(spectrum)
        rounded = spectrum.astype(BF16).reshape(half, degree_dev, share)
        gathered = [rounded] + [
            lax.ppermute(rounded, "lat", partner_pairs(lat_count, k)) for k in range(1, lat_count)
        ]
        coefs.append(inverse(chunk, gathered))
    total = jnp.zeros((8, 128), F32)
    for chunk in range(CHUNKS):
        total = zonal_values(chunk, swap_lon([coefs[chunk]] * lon_count), total)
    spectrum = jnp.concatenate(spectra, axis=3).transpose(2, 3, 0, 1)
    return (total.reshape(level_fields.shape), spectrum)


def solution(mesh):
    return jax.shard_map(
        shards,
        mesh=mesh,
        in_specs=(
            P(None, None, "lat", "lon"),
            P(None, None, "lat", "lon"),
            P("lat"),
            P("lat"),
            P("lon", "lat", None),
            P(),
            P(),
            P(),
        ),
        out_specs=(P(None, None, "lat", "lon"), P("lat", "lon", None, None)),
        check_vma=False,
    )
```

```python
import math

import jax
import jax.numpy as jnp
from jax import lax
from jax.experimental import pallas as pl
from jax.experimental.pallas import tpu as pltpu
from jax.sharding import PartitionSpec as P

NLON = 2560
M = 640


HIGHEST_PRECISION = lax.Precision.HIGHEST


def padded(cells, sides, width):
    for axis, dim in sides:
        count = lax.axis_size(axis)
        head = lax.slice_in_dim(cells, 0, width, axis=dim)
        tail = lax.slice_in_dim(cells, cells.shape[dim] - width, cells.shape[dim], axis=dim)
        cells = jnp.concatenate(
            [
                lax.ppermute(tail, axis, [(i, (i + 1) % count) for i in range(count)]),
                cells,
                lax.ppermute(head, axis, [((i + 1) % count, i) for i in range(count)]),
            ],
            axis=dim,
        )
    return cells


def angle_table(waves, columns):
    return (waves[:, None] * columns[None, :] % NLON).astype(jnp.float32) * (2.0 * math.pi / NLON)


def correct(spectrum, degrees, damping, vertical):
    modal = jnp.einsum("kl,nmcl->nmck", vertical, spectrum, precision=HIGHEST_PRECISION)
    divisor = 1.0 + damping[None, :] * (degrees * (degrees + 1)).astype(jnp.float32)[
        :, None
    ] / float(M * M)
    modal = modal / divisor[:, None, None, :]
    return jnp.einsum("kl,nmck->nmcl", vertical, modal, precision=HIGHEST_PRECISION)


def untiled(
    level_fields, wind_field, zonal_step, quad_weight, legendre, wave_table, damping, vertical
):
    levels, hemis, rows_half, lon_dev = level_fields.shape
    slots_dev = legendre.shape[0]
    lat_count = lax.axis_size("lat")
    lat_index = lax.axis_index("lat")
    lon_index = lax.axis_index("lon")
    degree_dev = M // lat_count
    grid_count = levels * hemis * rows_half
    contract_last = (((1,), (1,)), ((), ()))
    contract_first = (((0,), (0,)), ((), ()))
    batch_slots = (((2,), (1,)), ((0,), (0,)))
    extended = padded(level_fields, (("lat", 2), ("lon", 3)), 1)
    eastward = extended[:, :, 1:-1, 2:]
    westward = extended[:, :, 1:-1, :-2]
    toward = extended[:, :, 2:, 1:-1]
    poleward = extended[:, :, :-2, 1:-1]
    row_number = jnp.arange(rows_half)
    at_equator = (row_number == rows_half - 1) & (lat_index == lat_count - 1)
    toward = jnp.where(at_equator[:, None], level_fields[:, ::-1, -1:, :], toward)
    at_pole = (row_number == 0) & (lat_index == 0)
    poleward = jnp.where(at_pole[:, None], 0.0, poleward)
    tendency = wind_field[0] * zonal_step[:, None] * (eastward - westward) + 0.25 * wind_field[
        1
    ] * (toward - poleward)
    stepped = level_fields - tendency
    my_waves = lax.dynamic_slice_in_dim(wave_table, lon_index * slots_dev, slots_dev)
    portion = lax.all_gather(stepped, "lon", axis=3, tiled=True)
    lon_width = portion.shape[3]
    columns = jnp.arange(lon_width, dtype=jnp.int32)
    angles = angle_table(my_waves, columns)
    values = portion.reshape(grid_count, lon_width)
    cosine_sum = lax.dot_general(
        jnp.cos(angles), values, contract_last, precision=HIGHEST_PRECISION
    )
    sine_sum = lax.dot_general(jnp.sin(angles), values, contract_last, precision=HIGHEST_PRECISION)
    cosine_sum, sine_sum = (cosine_sum, sine_sum)
    fourier = jnp.stack([cosine_sum, -sine_sum], axis=1) / math.sqrt(NLON)
    weighted = (fourier.reshape(slots_dev, 2, levels, hemis, rows_half) * quad_weight).astype(
        jnp.bfloat16
    )
    weighted = weighted.reshape(slots_dev, 2 * levels * hemis, rows_half)
    table_part = legendre
    summed = lax.dot_general(weighted, table_part, batch_slots, preferred_element_type=jnp.float32)
    summed = summed.reshape(slots_dev, 2, levels, hemis, degree_dev * lax.axis_size("lat"))
    degrees = jnp.arange(degree_dev * lax.axis_size("lat"), dtype=jnp.int32)
    parity = jnp.where((degrees[None, :] - my_waves[:, None]) % 2 == 0, 1.0, -1.0)
    kept_mask = degrees[None, :] >= my_waves[:, None]
    combined = summed[:, :, :, 0] + parity[:, None, None, :] * summed[:, :, :, 1]
    combined = jnp.where(kept_mask[:, None, None, :], combined, 0.0)
    raw = lax.psum_scatter(combined.transpose(3, 0, 1, 2), "lat", scatter_dimension=0, tiled=True)
    my_degrees = lat_index * degree_dev + jnp.arange(degree_dev, dtype=jnp.int32)
    spectrum = correct(raw, my_degrees, damping, vertical)
    portion = lax.all_gather(spectrum.astype(jnp.bfloat16), "lat", axis=0, tiled=True)
    row_count = portion.shape[0]
    table_part = legendre
    degrees = jnp.arange(row_count, dtype=jnp.int32)
    even_mask = ((degrees[None, :] - my_waves[:, None]) % 2 == 0)[:, :, None]
    arranged = portion.transpose(1, 0, 2, 3).reshape(slots_dev, row_count, 2 * levels)
    even_sum = lax.dot_general(
        table_part,
        jnp.where(even_mask, arranged, 0),
        batch_slots,
        preferred_element_type=jnp.float32,
    )
    odd_sum = lax.dot_general(
        table_part,
        jnp.where(even_mask, 0, arranged),
        batch_slots,
        preferred_element_type=jnp.float32,
    )
    even_sum, odd_sum = (even_sum, odd_sum)
    coefs = jnp.stack([even_sum + odd_sum, even_sum - odd_sum], axis=1) / math.sqrt(M)
    coefs = (
        coefs.reshape(slots_dev, 2, rows_half, 2, levels)
        .transpose(0, 3, 4, 1, 2)
        .reshape(slots_dev, 2, grid_count)
    )
    my_columns = lon_index * lon_dev + jnp.arange(lon_dev, dtype=jnp.int32)
    portion = lax.all_gather(coefs, "lon", axis=0, tiled=True)
    factor = jnp.where(wave_table == 0, 1.0, 2.0)[:, None]
    angles = angle_table(wave_table, my_columns)
    totals = lax.dot_general(
        portion[:, 0], jnp.cos(angles) * factor, contract_first, precision=HIGHEST_PRECISION
    )
    grid_out = totals - lax.dot_general(
        portion[:, 1], jnp.sin(angles) * factor, contract_first, precision=HIGHEST_PRECISION
    )
    new_fields = (grid_out / math.sqrt(NLON)).reshape(level_fields.shape)
    return (new_fields, spectrum)


UNIT = 32
CUTS = (64, 96)
GROUP = 16
LANES = 128
F32 = jnp.float32
BF16 = jnp.bfloat16


def split_halves(value):
    high = value.astype(BF16)
    return high, (value - high.astype(F32)).astype(BF16)


def dot_rows(left, right):
    return lax.dot_general(left, right, (((1,), (1,)), ((), ())), preferred_element_type=F32)


def dot_columns(left, right):
    return lax.dot_general(left, right, (((0,), (0,)), ((), ())), preferred_element_type=F32)


def pairs(count, step):
    return [(i, i ^ step) for i in range(count)]


def edges_kernel(fields_ref, first_row, last_row, first_column, last_column):
    count, rows, columns = fields_ref.shape
    for p in range(count):
        first_row[p : p + 1, :] = fields_ref[p, 0:1, :]
        last_row[p : p + 1, :] = fields_ref[p, rows - 1 : rows, :]
        first_column[:, p : p + 1] = fields_ref[p, :, 0:1]
        last_column[:, p : p + 1] = fields_ref[p, :, columns - 1 : columns]


def advance(flags, fields_ref, wind_ref, step_ref, above, below, before, after, stepped_ref):
    count, rows, columns = fields_ref.shape
    lane = lax.broadcasted_iota(jnp.int32, (rows, columns), 1)
    row = lax.broadcasted_iota(jnp.int32, (rows, columns), 0)
    for p in range(count):
        h = p % 2
        field = fields_ref[p]
        eastward = jnp.where(
            lane == columns - 1, after[:, p : p + 1], pltpu.roll(field, columns - 1, 1)
        )
        westward = jnp.where(lane == 0, before[:, p : p + 1], pltpu.roll(field, 1, 1))
        other = fields_ref[p ^ 1, rows - 1 : rows, :]
        low_edge = jnp.where(flags[1] == 1, other, below[p : p + 1, :])
        high_edge = jnp.where(flags[0] == 1, 0.0, above[p : p + 1, :])
        toward = jnp.where(row == rows - 1, low_edge, pltpu.roll(field, rows - 1, 0))
        poleward = jnp.where(row == 0, high_edge, pltpu.roll(field, 1, 0))
        tendency = wind_ref[h] * step_ref[...] * (eastward - westward) + 0.25 * wind_ref[
            2 + h
        ] * (toward - poleward)
        stepped_ref[p * rows : (p + 1) * rows, :] = field - tendency


def table_rows(near, far, first, share, blocks, part):
    per_block = near.shape[0] // blocks
    half = far.shape[1] // 2
    out = []
    for k in range(blocks):
        at = pl.ds(k * per_block + first, share)
        near_cos, near_sin = near[at, :LANES], near[at, LANES:]
        far_cos, far_sin = far[at, :half], far[at, half:]
        columns = []
        for j in range(half):
            c, s = far_cos[:, j : j + 1], far_sin[:, j : j + 1]
            if part:
                columns.append(-(s * near_cos + c * near_sin))
            else:
                columns.append(c * near_cos - s * near_sin)
        out.append(jnp.concatenate(columns, axis=1))
    return jnp.concatenate(out, axis=0)


def zonal_sums(blocks, share, first, stepped_ref, near, far, outs):
    high, low = split_halves(stepped_ref[...])
    count = stepped_ref.shape[0]
    for part in range(2):
        rows_high, rows_low = split_halves(table_rows(near, far, first, share, blocks, part))
        sums = dot_rows(rows_high, high) + (dot_rows(rows_high, low) + dot_rows(rows_low, high))
        for k, out in enumerate(outs):
            out[:, part * count : (part + 1) * count] = sums[
                k * share : (k + 1) * share, :
            ].astype(out.dtype)


def forward_kernel(
    blocks, sections, rows, degree_dev, last, waves_ref, place_ref, *refs
):
    received = refs[:blocks]
    weight_ref, table_ref = refs[blocks : blocks + 2]
    rest = refs[blocks + 2 :]
    spread_ref, kept_ref, turned_ref = rest[-3:]
    step = pl.program_id(0)
    half = sections // 2
    levels = half // 2
    group = table_ref.shape[0]
    columns = table_ref.shape[2]
    share = spread_ref.shape[0]

    @pl.when(step == 0)
    def _():
        total = received[0][...].astype(F32)
        for other in received[1:]:
            total = total + other[...].astype(F32)
        total = total * weight_ref[...]
        for c in range(2):
            for level in range(levels):
                for h in range(2):
                    at = ((c * levels + level) * 2 + h) * rows
                    spread_ref[:, h * half + level * 2 + c, 0:rows] = total[:, at : at + rows]

    degree = lax.broadcasted_iota(jnp.int32, (2 * half, columns), 1)
    row = lax.broadcasted_iota(jnp.int32, (2 * half, 1), 0)
    for u in range(0, group, 2):
        sums = []
        for v in (u, u + 1):
            high, low = split_halves(spread_ref[step * group + v, :, 0:rows])
            both = jnp.concatenate([high.astype(F32), low.astype(F32)], axis=0).astype(BF16)
            total = jnp.dot(both, table_ref[v], preferred_element_type=F32)
            sums.append(total[:sections] + total[sections:])
        north = jnp.concatenate([sums[0][:half], sums[1][:half]], axis=0)
        south = jnp.concatenate([sums[0][half:], sums[1][half:]], axis=0)
        slot = step * group + u
        past = degree - jnp.where(row < half, waves_ref[slot], waves_ref[slot + 1])
        combined = north + jnp.where(past & 1 == 0, south, -south)
        combined = jnp.where(past >= 0, combined, 0.0)
        at = pl.ds(pl.multiple_of(slot * half, 2 * half), 2 * half)
        for t in range(columns // LANES):
            kept_ref[t, at, :] = combined[:, t * LANES : (t + 1) * LANES]

    @pl.when(step == pl.num_programs(0) - 1)
    def _():
        target = turned_ref if last else rest[0]
        for t in range(columns // LANES):
            tile = jnp.concatenate(
                [kept_ref[t, pl.ds(j, share, stride=half), :] for j in range(half)], axis=0
            )
            target[t * LANES : (t + 1) * LANES, :] = tile.T
        if not last:
            return
        earlier, (own_ref, other_ref) = rest[:-5], rest[-5:-3]
        for j in range(own_ref.shape[0]):
            for out, k in ((own_ref, 2 * j), (other_ref, 2 * j + 1)):
                at = pl.ds(pl.multiple_of((place_ref[0] ^ k) * degree_dev, 8), degree_dev)
                done = 0
                for source in (*earlier, turned_ref):
                    wide = source.shape[1]
                    out[j, :, done : done + wide] = source[at, :]
                    done += wide


def correct_kernel(
    cuts, levels, place_ref, damping_ref, vertical_ref, sum_ref, *refs
):
    others, (rounded_ref, spectrum_ref) = refs[:-2], refs[-2:]
    total = sum_ref[...]
    for other in others:
        total = total + other[...].astype(F32)
    count = total.shape[0]
    degree = place_ref[0] * count + lax.broadcasted_iota(jnp.int32, (count, 1), 0)
    growth = (degree * (degree + 1)).astype(F32) / float(M * M)
    scale = [1.0 / (1.0 + damping_ref[k] * growth) for k in range(levels)]
    at, slot = 0, 0
    for share in cuts:
        wide = 2 * share
        raw = [total[:, at + l * wide : at + (l + 1) * wide] for l in range(levels)]
        modal = [
            sum(vertical_ref[k, l] * raw[l] for l in range(levels)) * scale[k]
            for k in range(levels)
        ]
        for l in range(levels):
            value = sum(vertical_ref[k, l] * modal[k] for k in range(levels))
            rounded_ref[:, at + l * wide : at + (l + 1) * wide] = value.astype(BF16)
            for c in range(2):
                spectrum_ref[c * levels + l, :, slot : slot + share] = value[
                    :, c * share : (c + 1) * share
                ]
        at, slot = at + levels * wide, slot + share


def inverse_kernel(sections, rows, first, waves_ref, joined_ref, table_ref, out_ref, kept_ref, spread_ref):
    step = pl.program_id(0)
    half = sections // 2
    levels = half // 2
    group = table_ref.shape[0]
    columns = table_ref.shape[2]
    share = spread_ref.shape[0]

    @pl.when(step == 0)
    def _():
        for t in range(columns // LANES):
            tile = joined_ref[t * LANES : (t + 1) * LANES, half * first : half * (first + share)]
            turned = tile.astype(F32).T
            for j in range(half):
                kept_ref[t, pl.ds(j, share, stride=half), :] = turned[
                    j * share : (j + 1) * share, :
                ]

    degree = lax.broadcasted_iota(jnp.int32, (2 * half, columns), 1)
    row = lax.broadcasted_iota(jnp.int32, (2 * half, 1), 0)
    upper = row < half
    for u in range(0, group, 2):
        slot = step * group + u
        at = pl.ds(pl.multiple_of(slot * half, 2 * half), 2 * half)
        values = jnp.concatenate(
            [kept_ref[t, at, :] for t in range(columns // LANES)], axis=1
        )
        even = (degree - jnp.where(upper, waves_ref[slot], waves_ref[slot + 1])) & 1 == 0
        evens = jnp.where(even, values, 0.0)
        odds = pltpu.roll(jnp.where(even, 0.0, values), half, 0)
        for v in range(2):
            both = jnp.where(upper, odds, evens) if v else jnp.where(upper, evens, odds)
            sums = dot_rows(both.astype(BF16), table_ref[u + v])
            factor = jnp.where(waves_ref[slot + v] == 0, 1.0, 2.0) / math.sqrt(M)
            sums = sums * factor
            swapped = pltpu.roll(sums, half, 0)
            less = sums - swapped if v else swapped - sums
            spread_ref[slot + v, :, 0:rows] = jnp.where(upper, sums + swapped, less)

    @pl.when(step == pl.num_programs(0) - 1)
    def _():
        for c in range(2):
            for level in range(levels):
                for h in range(2):
                    at = ((c * levels + level) * 2 + h) * rows
                    out_ref[:, at : at + rows] = spread_ref[
                        :, h * half + level * 2 + c, 0:rows
                    ].astype(out_ref.dtype)


def zonal_values(blocks, share, first, near, far, received, total):
    for part in range(2):
        count = received[0].shape[1] // 2
        rows_high, rows_low = split_halves(table_rows(near, far, first, share, blocks, part))
        coefs = jnp.concatenate(
            [other[:, part * count : (part + 1) * count] for other in received], axis=0
        )
        term = dot_columns(coefs, rows_high) + dot_columns(coefs, rows_low)
        total = term if total is None else total + term
    return total


VMEM = pl.BlockSpec(memory_space=pltpu.VMEM)
SMEM = pl.BlockSpec(memory_space=pltpu.SMEM)


def grant(size):
    return pltpu.CompilerParams(vmem_limit_bytes=size << 20)


def like(shape, dtype):
    return jax.ShapeDtypeStruct(shape, dtype)


def whole_block(shape):
    return pl.BlockSpec(shape, lambda *_: (0,) * len(shape))


def shards(
    level_fields, wind_field, zonal_step, quad_weight, legendre, wave_table, damping, vertical
):
    levels, hemis, rows_half, lon_dev = level_fields.shape
    slots_dev, _, columns = legendre.shape
    lat_count = lax.axis_size("lat")
    lon_count = lax.axis_size("lon")
    degree_dev = columns // lat_count
    if (
        rows_half % 16
        or degree_dev % 16
        or lon_dev % LANES
        or slots_dev != sum(CUTS)
        or levels != 2
        or lat_count & (lat_count - 1)
        or lat_count < 4
        or lon_count & (lon_count - 1)
    ):
        return untiled(
            level_fields,
            wind_field,
            zonal_step,
            quad_weight,
            legendre,
            wave_table,
            damping,
            vertical,
        )
    lat_index = lax.axis_index("lat")
    lon_index = lax.axis_index("lon")
    planes = levels * hemis
    grid_count = planes * rows_half
    sections = 2 * planes
    half = sections // 2
    width = 2 * grid_count
    fields = level_fields.reshape(planes, rows_half, lon_dev)
    winds = wind_field.reshape(2 * hemis, rows_half, lon_dev)

    first_row, last_row, first_column, last_column = pl.pallas_call(
        edges_kernel,
        out_shape=[like((planes, lon_dev), F32)] * 2 + [like((rows_half, planes), F32)] * 2,
        in_specs=[VMEM],
        out_specs=[VMEM] * 4,
        compiler_params=grant(8),
        name="edges",
    )(fields)
    up = [(i, (i + 1) % lat_count) for i in range(lat_count)]
    east = [(i, (i + 1) % lon_count) for i in range(lon_count)]
    down = [(j, i) for i, j in up]
    west = [(j, i) for i, j in east]
    above = lax.ppermute(last_row, "lat", up)
    below = lax.ppermute(first_row, "lat", down)
    before = lax.ppermute(last_column, "lon", east)
    after = lax.ppermute(first_column, "lon", west)

    order = [
        lax.dynamic_slice_in_dim(wave_table, (lon_index ^ k) * slots_dev, slots_dev)
        for k in range(lon_count)
    ]
    my_waves = order[0]
    waves = jnp.concatenate(order)
    near_angle = angle_table(waves, jnp.arange(LANES, dtype=jnp.int32))
    near = jnp.concatenate([jnp.cos(near_angle), jnp.sin(near_angle)], axis=1)
    far_angle = angle_table(
        waves, lon_index * lon_dev + LANES * jnp.arange(lon_dev // LANES, dtype=jnp.int32)
    )
    far = jnp.concatenate([jnp.cos(far_angle), jnp.sin(far_angle)], axis=1) / math.sqrt(NLON)

    flags = jnp.stack([lat_index == 0, lat_index == lat_count - 1]).astype(jnp.int32)
    place = lat_index.astype(jnp.int32).reshape(1)
    weight_row = jnp.tile(quad_weight, sections)[None, :]

    def sums_shape(share):
        return [like((share, width), BF16 if k else F32) for k in range(lon_count)]

    def first_sums(flags_ref, fields_ref, winds_ref, step_ref, *refs):
        edges, near_ref, far_ref, stepped_ref = refs[:4], refs[4], refs[5], refs[6]
        advance(flags_ref, fields_ref, winds_ref, step_ref, *edges, stepped_ref)
        zonal_sums(lon_count, CUTS[0], 0, stepped_ref, near_ref, far_ref, refs[7:])

    stepped, *pieces = pl.pallas_call(
        first_sums,
        out_shape=[like((grid_count, lon_dev), F32)] + sums_shape(CUTS[0]),
        in_specs=[SMEM] + [VMEM] * 9,
        out_specs=[VMEM] * (1 + lon_count),
        compiler_params=grant(24),
        name="advance_and_sums",
    )(flags, fields, winds, zonal_step[:, None], above, below, before, after, near, far)

    def later_sums(share, first):
        def body(stepped_ref, near_ref, far_ref, *outs):
            zonal_sums(lon_count, share, first, stepped_ref, near_ref, far_ref, outs)

        return pl.pallas_call(
            body,
            out_shape=sums_shape(share),
            in_specs=[VMEM] * 3,
            out_specs=[VMEM] * lon_count,
            compiler_params=grant(24),
            name="sums",
        )(stepped, near, far)

    def swap_lon(parts):
        return [parts[0]] + [
            lax.ppermute(parts[k], "lon", pairs(lon_count, k)) for k in range(1, lon_count)
        ]

    swapped, first = [swap_lon(pieces)], CUTS[0]
    for share in CUTS[1:]:
        swapped.append(swap_lon(later_sums(share, first)))
        first += share

    def table_spec(first):
        return pl.BlockSpec(
            (GROUP, rows_half, columns), lambda g, *_: (first // GROUP + g, 0, 0)
        )

    def forward(first, share, parts, earlier, last):
        if last:
            shape = (lat_count // 2, degree_dev, half * slots_dev)
            shapes = [like(shape, F32)] * 2
        else:
            shapes = [like((columns, half * share), F32)]
        return pl.pallas_call(
            lambda *refs: forward_kernel(
                lon_count, sections, rows_half, degree_dev, last, *refs
            ),
            out_shape=shapes,
            grid_spec=pltpu.PrefetchScalarGridSpec(
                num_scalar_prefetch=2,
                grid=(share // GROUP,),
                in_specs=[whole_block((share, width))] * lon_count
                + [whole_block((1, width)), table_spec(first)]
                + [whole_block(other.shape) for other in earlier],
                out_specs=[whole_block(shape.shape) for shape in shapes],
                scratch_shapes=[
                    pltpu.VMEM((share, sections, LANES), F32),
                    pltpu.VMEM((columns // LANES, half * share, LANES), F32),
                    pltpu.VMEM((columns, half * share), F32),
                ],
            ),
            compiler_params=grant(50),
            name="forward",
        )(my_waves[first : first + share], place, *parts, weight_row, legendre, *earlier)

    earlier, first = [], 0
    for share, parts in zip(CUTS, swapped):
        last = first + share == slots_dev
        earlier = earlier + list(forward(first, share, parts, earlier if last else [], last))
        first += share
    own, other = earlier[-2:]

    other = lax.ppermute(other, "lat", pairs(lat_count, 1))
    sums = [own[j] + other[j] for j in range(lat_count // 2)]
    sums = [sums[0]] + [
        lax.ppermute(sums[j].astype(BF16), "lat", pairs(lat_count, 2 * j))
        for j in range(1, lat_count // 2)
    ]
    rounded, spectrum = pl.pallas_call(
        lambda *refs: correct_kernel(CUTS, levels, *refs),
        out_shape=[
            like((degree_dev, half * slots_dev), BF16),
            like((half, degree_dev, slots_dev), F32),
        ],
        in_specs=[SMEM] * 3 + [VMEM] * len(sums),
        out_specs=[VMEM] * 2,
        compiler_params=grant(8),
        name="correct",
    )(place, damping, vertical, *sums)
    joined = lax.all_gather(rounded, "lat", axis=0, tiled=True)

    def inverse(first, share):
        return pl.pallas_call(
            lambda *refs: inverse_kernel(sections, rows_half, first, *refs),
            out_shape=like((share, width), BF16),
            grid_spec=pltpu.PrefetchScalarGridSpec(
                num_scalar_prefetch=1,
                grid=(share // GROUP,),
                in_specs=[whole_block(joined.shape), table_spec(first)],
                out_specs=whole_block((share, width)),
                scratch_shapes=[
                    pltpu.VMEM((columns // LANES, half * share, LANES), F32),
                    pltpu.VMEM((share, sections, LANES), F32),
                ],
            ),
            compiler_params=grant(50),
            name="inverse",
        )(my_waves[first : first + share], joined, legendre)

    def values(first, share, parts, base):
        def body(near_ref, far_ref, *refs):
            start = refs[lon_count][...] if base else None
            refs[-1][...] = zonal_values(
                lon_count, share, first, near_ref, far_ref, refs[:lon_count], start
            )

        return pl.pallas_call(
            body,
            out_shape=like((grid_count, lon_dev), F32),
            in_specs=[VMEM] * (2 + lon_count + len(base)),
            out_specs=VMEM,
            compiler_params=grant(24),
            name="values",
        )(near, far, *parts, *base)

    base, first = [], 0
    for share in CUTS:
        coefs = inverse(first, share)
        base = [values(first, share, swap_lon([coefs] * lon_count), base)]
        first += share
    spectrum = spectrum.reshape(2, levels, degree_dev, slots_dev).transpose(2, 3, 0, 1)
    return (base[0].reshape(level_fields.shape), spectrum)


def solution(mesh):
    return jax.shard_map(
        shards,
        mesh=mesh,
        in_specs=(
            P(None, None, "lat", "lon"),
            P(None, None, "lat", "lon"),
            P("lat"),
            P("lat"),
            P("lon", "lat", None),
            P(),
            P(),
            P(),
        ),
        out_specs=(P(None, None, "lat", "lon"), P("lat", "lon", None, None)),
        check_vma=False,
    )
```

```python
import math

import jax
import jax.numpy as jnp
from jax import lax
from jax.experimental import pallas as pl
from jax.experimental.pallas import tpu as pltpu
from jax.sharding import PartitionSpec as P

NLON = 2560
M = 640


HIGHEST_PRECISION = lax.Precision.HIGHEST


def padded(cells, sides, width):
    for axis, dim in sides:
        count = lax.axis_size(axis)
        head = lax.slice_in_dim(cells, 0, width, axis=dim)
        tail = lax.slice_in_dim(cells, cells.shape[dim] - width, cells.shape[dim], axis=dim)
        cells = jnp.concatenate(
            [
                lax.ppermute(tail, axis, [(i, (i + 1) % count) for i in range(count)]),
                cells,
                lax.ppermute(head, axis, [((i + 1) % count, i) for i in range(count)]),
            ],
            axis=dim,
        )
    return cells


def angle_table(waves, columns):
    return (waves[:, None] * columns[None, :] % NLON).astype(jnp.float32) * (2.0 * math.pi / NLON)


def correct(spectrum, degrees, damping, vertical):
    modal = jnp.einsum("kl,nmcl->nmck", vertical, spectrum, precision=HIGHEST_PRECISION)
    divisor = 1.0 + damping[None, :] * (degrees * (degrees + 1)).astype(jnp.float32)[
        :, None
    ] / float(M * M)
    modal = modal / divisor[:, None, None, :]
    return jnp.einsum("kl,nmck->nmcl", vertical, modal, precision=HIGHEST_PRECISION)


def untiled(
    level_fields, wind_field, zonal_step, quad_weight, legendre, wave_table, damping, vertical
):
    levels, hemis, rows_half, lon_dev = level_fields.shape
    slots_dev = legendre.shape[0]
    lat_count = lax.axis_size("lat")
    lat_index = lax.axis_index("lat")
    lon_index = lax.axis_index("lon")
    degree_dev = M // lat_count
    grid_count = levels * hemis * rows_half
    contract_last = (((1,), (1,)), ((), ()))
    contract_first = (((0,), (0,)), ((), ()))
    batch_slots = (((2,), (1,)), ((0,), (0,)))
    extended = padded(level_fields, (("lat", 2), ("lon", 3)), 1)
    eastward = extended[:, :, 1:-1, 2:]
    westward = extended[:, :, 1:-1, :-2]
    toward = extended[:, :, 2:, 1:-1]
    poleward = extended[:, :, :-2, 1:-1]
    row_number = jnp.arange(rows_half)
    at_equator = (row_number == rows_half - 1) & (lat_index == lat_count - 1)
    toward = jnp.where(at_equator[:, None], level_fields[:, ::-1, -1:, :], toward)
    at_pole = (row_number == 0) & (lat_index == 0)
    poleward = jnp.where(at_pole[:, None], 0.0, poleward)
    tendency = wind_field[0] * zonal_step[:, None] * (eastward - westward) + 0.25 * wind_field[
        1
    ] * (toward - poleward)
    stepped = level_fields - tendency
    my_waves = lax.dynamic_slice_in_dim(wave_table, lon_index * slots_dev, slots_dev)
    portion = lax.all_gather(stepped, "lon", axis=3, tiled=True)
    lon_width = portion.shape[3]
    columns = jnp.arange(lon_width, dtype=jnp.int32)
    angles = angle_table(my_waves, columns)
    values = portion.reshape(grid_count, lon_width)
    cosine_sum = lax.dot_general(
        jnp.cos(angles), values, contract_last, precision=HIGHEST_PRECISION
    )
    sine_sum = lax.dot_general(jnp.sin(angles), values, contract_last, precision=HIGHEST_PRECISION)
    cosine_sum, sine_sum = (cosine_sum, sine_sum)
    fourier = jnp.stack([cosine_sum, -sine_sum], axis=1) / math.sqrt(NLON)
    weighted = (fourier.reshape(slots_dev, 2, levels, hemis, rows_half) * quad_weight).astype(
        jnp.bfloat16
    )
    weighted = weighted.reshape(slots_dev, 2 * levels * hemis, rows_half)
    table_part = legendre
    summed = lax.dot_general(weighted, table_part, batch_slots, preferred_element_type=jnp.float32)
    summed = summed.reshape(slots_dev, 2, levels, hemis, degree_dev * lax.axis_size("lat"))
    degrees = jnp.arange(degree_dev * lax.axis_size("lat"), dtype=jnp.int32)
    parity = jnp.where((degrees[None, :] - my_waves[:, None]) % 2 == 0, 1.0, -1.0)
    kept_mask = degrees[None, :] >= my_waves[:, None]
    combined = summed[:, :, :, 0] + parity[:, None, None, :] * summed[:, :, :, 1]
    combined = jnp.where(kept_mask[:, None, None, :], combined, 0.0)
    raw = lax.psum_scatter(combined.transpose(3, 0, 1, 2), "lat", scatter_dimension=0, tiled=True)
    my_degrees = lat_index * degree_dev + jnp.arange(degree_dev, dtype=jnp.int32)
    spectrum = correct(raw, my_degrees, damping, vertical)
    portion = lax.all_gather(spectrum.astype(jnp.bfloat16), "lat", axis=0, tiled=True)
    row_count = portion.shape[0]
    table_part = legendre
    degrees = jnp.arange(row_count, dtype=jnp.int32)
    even_mask = ((degrees[None, :] - my_waves[:, None]) % 2 == 0)[:, :, None]
    arranged = portion.transpose(1, 0, 2, 3).reshape(slots_dev, row_count, 2 * levels)
    even_sum = lax.dot_general(
        table_part,
        jnp.where(even_mask, arranged, 0),
        batch_slots,
        preferred_element_type=jnp.float32,
    )
    odd_sum = lax.dot_general(
        table_part,
        jnp.where(even_mask, 0, arranged),
        batch_slots,
        preferred_element_type=jnp.float32,
    )
    even_sum, odd_sum = (even_sum, odd_sum)
    coefs = jnp.stack([even_sum + odd_sum, even_sum - odd_sum], axis=1) / math.sqrt(M)
    coefs = (
        coefs.reshape(slots_dev, 2, rows_half, 2, levels)
        .transpose(0, 3, 4, 1, 2)
        .reshape(slots_dev, 2, grid_count)
    )
    my_columns = lon_index * lon_dev + jnp.arange(lon_dev, dtype=jnp.int32)
    portion = lax.all_gather(coefs, "lon", axis=0, tiled=True)
    factor = jnp.where(wave_table == 0, 1.0, 2.0)[:, None]
    angles = angle_table(wave_table, my_columns)
    totals = lax.dot_general(
        portion[:, 0], jnp.cos(angles) * factor, contract_first, precision=HIGHEST_PRECISION
    )
    grid_out = totals - lax.dot_general(
        portion[:, 1], jnp.sin(angles) * factor, contract_first, precision=HIGHEST_PRECISION
    )
    new_fields = (grid_out / math.sqrt(NLON)).reshape(level_fields.shape)
    return (new_fields, spectrum)


CUTS = (64, 64, 32)
GROUP = 16
LANES = 128
F32 = jnp.float32
BF16 = jnp.bfloat16


def split_halves(value):
    high = value.astype(BF16)
    return high, (value - high.astype(F32)).astype(BF16)


def dot_rows(left, right):
    return lax.dot_general(left, right, (((1,), (1,)), ((), ())), preferred_element_type=F32)


def dot_columns(left, right):
    return lax.dot_general(left, right, (((0,), (0,)), ((), ())), preferred_element_type=F32)


def pairs(count, step):
    return [(i, i ^ step) for i in range(count)]


def load_kernel(fields_hbm, winds_hbm, fields_ref, winds_ref, *refs):
    first_row, last_row, first_column, last_column, semaphores = refs
    fields_copy = pltpu.make_async_copy(fields_hbm, fields_ref, semaphores.at[0])
    winds_copy = pltpu.make_async_copy(winds_hbm, winds_ref, semaphores.at[1])
    fields_copy.start()
    winds_copy.start()
    fields_copy.wait()
    count, rows, columns = fields_ref.shape
    for p in range(count):
        first_row[p : p + 1, :] = fields_ref[p, 0:1, :]
        last_row[p : p + 1, :] = fields_ref[p, rows - 1 : rows, :]
        first_column[:, p : p + 1] = fields_ref[p, :, 0:1]
        last_column[:, p : p + 1] = fields_ref[p, :, columns - 1 : columns]
    winds_copy.wait()


def load_table_kernel(after_ref, table_hbm, table_ref, semaphores):
    parts = semaphores.shape[0]
    share = table_ref.shape[0] // parts
    copies = [
        pltpu.make_async_copy(
            table_hbm.at[pl.ds(i * share, share)],
            table_ref.at[pl.ds(i * share, share)],
            semaphores.at[i],
        )
        for i in range(parts)
    ]
    for copy in copies:
        copy.start()
    for copy in copies:
        copy.wait()


def advance(flags, fields_ref, wind_ref, step_ref, above, below, before, after, stepped_ref):
    count, rows, columns = fields_ref.shape
    lane = lax.broadcasted_iota(jnp.int32, (rows, columns), 1)
    row = lax.broadcasted_iota(jnp.int32, (rows, columns), 0)
    square = (rows, rows)
    diagonal = lax.broadcasted_iota(jnp.int32, square, 0) == lax.broadcasted_iota(
        jnp.int32, square, 1
    )
    steps = jnp.sum(jnp.where(diagonal, step_ref[...], 0.0), axis=1, keepdims=True)
    for p in range(count):
        h = p % 2
        field = fields_ref[p]
        eastward = jnp.where(
            lane == columns - 1, after[:, p : p + 1], pltpu.roll(field, columns - 1, 1)
        )
        westward = jnp.where(lane == 0, before[:, p : p + 1], pltpu.roll(field, 1, 1))
        other = fields_ref[p ^ 1, rows - 1 : rows, :]
        low_edge = jnp.where(flags[1] == 1, other, below[p : p + 1, :])
        high_edge = jnp.where(flags[0] == 1, 0.0, above[p : p + 1, :])
        toward = jnp.where(row == rows - 1, low_edge, pltpu.roll(field, rows - 1, 0))
        poleward = jnp.where(row == 0, high_edge, pltpu.roll(field, 1, 0))
        tendency = wind_ref[h] * steps * (eastward - westward) + 0.25 * wind_ref[
            2 + h
        ] * (toward - poleward)
        stepped_ref[p * rows : (p + 1) * rows, :] = field - tendency


def table_rows(near, far, first, share, blocks, part):
    per_block = near.shape[0] // blocks
    half = far.shape[1] // 2
    out = []
    for k in range(blocks):
        at = pl.ds(k * per_block + first, share)
        near_cos, near_sin = near[at, :LANES], near[at, LANES:]
        far_cos, far_sin = far[at, :half], far[at, half:]
        columns = []
        for j in range(half):
            c, s = far_cos[:, j : j + 1], far_sin[:, j : j + 1]
            if part:
                columns.append(-(s * near_cos + c * near_sin))
            else:
                columns.append(c * near_cos - s * near_sin)
        out.append(jnp.concatenate(columns, axis=1))
    return jnp.concatenate(out, axis=0)


def zonal_sums(blocks, share, first, stepped_ref, near, far, outs):
    high, low = split_halves(stepped_ref[...])
    count = stepped_ref.shape[0]
    for part in range(2):
        rows_high, rows_low = split_halves(table_rows(near, far, first, share, blocks, part))
        sums = dot_rows(rows_high, high) + (dot_rows(rows_high, low) + dot_rows(rows_low, high))
        lanes = slice(part * count, (part + 1) * count)
        own, pair = outs
        for k in range(0, blocks, 2):
            own[k // 2, :, lanes] = sums[k * share : (k + 1) * share, :]
            pair[k // 2, :, lanes] = sums[(k + 1) * share : (k + 2) * share, :].astype(BF16)


def forward_kernel(
    blocks, sections, rows, degree_dev, first, last, waves_ref, place_ref, *refs
):
    received = refs[:blocks]
    weight_ref, table_ref = refs[blocks : blocks + 2]
    rest = refs[blocks + 2 :]
    spread_ref, kept_ref, turned_ref = rest[-3:]
    step = pl.program_id(0)
    half = sections // 2
    levels = half // 2
    group = GROUP
    columns = table_ref.shape[2]
    share = spread_ref.shape[0]

    @pl.when(step == 0)
    def _():
        total = received[0][...].astype(F32)
        for other in received[1:]:
            total = total + other[...].astype(F32)
        total = total * weight_ref[...]
        for c in range(2):
            for level in range(levels):
                for h in range(2):
                    at = ((c * levels + level) * 2 + h) * rows
                    spread_ref[:, h * half + level * 2 + c, 0:rows] = total[:, at : at + rows]

    degree = lax.broadcasted_iota(jnp.int32, (2 * half, columns), 1)
    row = lax.broadcasted_iota(jnp.int32, (2 * half, 1), 0)
    for u in range(0, group, 2):
        sums = []
        for v in (u, u + 1):
            high, low = split_halves(spread_ref[step * group + v, :, 0:rows])
            both = jnp.concatenate([high.astype(F32), low.astype(F32)], axis=0).astype(BF16)
            total = jnp.dot(both, table_ref[first + step * group + v], preferred_element_type=F32)
            sums.append(total[:sections] + total[sections:])
        north = jnp.concatenate([sums[0][:half], sums[1][:half]], axis=0)
        south = jnp.concatenate([sums[0][half:], sums[1][half:]], axis=0)
        slot = step * group + u
        past = degree - jnp.where(row < half, waves_ref[slot], waves_ref[slot + 1])
        combined = north + jnp.where(past & 1 == 0, south, -south)
        combined = jnp.where(past >= 0, combined, 0.0)
        at = pl.ds(pl.multiple_of(slot * half, 2 * half), 2 * half)
        for t in range(columns // LANES):
            kept_ref[t, at, :] = combined[:, t * LANES : (t + 1) * LANES]

    @pl.when(step == pl.num_programs(0) - 1)
    def _():
        target = turned_ref if last else rest[-4]
        for t in range(columns // LANES):
            tile = jnp.concatenate(
                [kept_ref[t, pl.ds(j, share, stride=half), :] for j in range(half)], axis=0
            )
            target[t * LANES : (t + 1) * LANES, :] = tile.T
        if not last:
            return
        earlier, (own_ref, other_ref) = rest[:-5], rest[-5:-3]
        for j in range(own_ref.shape[0]):
            for out, k in ((own_ref, 2 * j), (other_ref, 2 * j + 1)):
                at = pl.ds(pl.multiple_of((place_ref[0] ^ k) * degree_dev, 8), degree_dev)
                done = 0
                for source in (*earlier, turned_ref):
                    wide = source.shape[1]
                    out[j, :, done : done + wide] = source[at, :]
                    done += wide


def correct_kernel(
    cuts, levels, place_ref, damping_ref, vertical_ref, sum_ref, *refs
):
    others, (rounded_ref, spectrum_ref) = refs[:-2], refs[-2:]
    total = sum_ref[...]
    for other in others:
        total = total + other[...].astype(F32)
    count = total.shape[0]
    degree = place_ref[0] * count + lax.broadcasted_iota(jnp.int32, (count, 1), 0)
    growth = (degree * (degree + 1)).astype(F32) / float(M * M)
    scale = [1.0 / (1.0 + damping_ref[k] * growth) for k in range(levels)]
    at, slot = 0, 0
    for share in cuts:
        wide = 2 * share
        raw = [total[:, at + l * wide : at + (l + 1) * wide] for l in range(levels)]
        modal = [
            sum(vertical_ref[k, l] * raw[l] for l in range(levels)) * scale[k]
            for k in range(levels)
        ]
        for l in range(levels):
            value = sum(vertical_ref[k, l] * modal[k] for k in range(levels))
            rounded_ref[:, at + l * wide : at + (l + 1) * wide] = value.astype(BF16)
            for c in range(2):
                spectrum_ref[c * levels + l, :, slot : slot + share] = value[
                    :, c * share : (c + 1) * share
                ]
        at, slot = at + levels * wide, slot + share


def inverse_kernel(sections, rows, first, waves_ref, joined_ref, table_ref, out_ref, kept_ref, spread_ref):
    step = pl.program_id(0)
    half = sections // 2
    levels = half // 2
    group = GROUP
    columns = table_ref.shape[2]
    share = spread_ref.shape[0]

    @pl.when(step == 0)
    def _():
        for t in range(columns // LANES):
            tile = joined_ref[t * LANES : (t + 1) * LANES, half * first : half * (first + share)]
            turned = tile.astype(F32).T
            for j in range(half):
                kept_ref[t, pl.ds(j, share, stride=half), :] = turned[
                    j * share : (j + 1) * share, :
                ]

    degree = lax.broadcasted_iota(jnp.int32, (2 * half, columns), 1)
    row = lax.broadcasted_iota(jnp.int32, (2 * half, 1), 0)
    upper = row < half
    for u in range(0, group, 2):
        slot = step * group + u
        at = pl.ds(pl.multiple_of(slot * half, 2 * half), 2 * half)
        values = jnp.concatenate(
            [kept_ref[t, at, :] for t in range(columns // LANES)], axis=1
        )
        even = (degree - jnp.where(upper, waves_ref[slot], waves_ref[slot + 1])) & 1 == 0
        evens = jnp.where(even, values, 0.0)
        odds = pltpu.roll(jnp.where(even, 0.0, values), half, 0)
        for v in range(2):
            both = jnp.where(upper, odds, evens) if v else jnp.where(upper, evens, odds)
            sums = dot_rows(both.astype(BF16), table_ref[first + slot + v])
            factor = jnp.where(waves_ref[slot + v] == 0, 1.0, 2.0) / math.sqrt(M)
            sums = sums * factor
            swapped = pltpu.roll(sums, half, 0)
            less = sums - swapped if v else swapped - sums
            spread_ref[slot + v, :, 0:rows] = jnp.where(upper, sums + swapped, less)

    @pl.when(step == pl.num_programs(0) - 1)
    def _():
        for c in range(2):
            for level in range(levels):
                for h in range(2):
                    at = ((c * levels + level) * 2 + h) * rows
                    out_ref[:, at : at + rows] = spread_ref[
                        :, h * half + level * 2 + c, 0:rows
                    ].astype(out_ref.dtype)


def zonal_values(blocks, share, first, near, far, received, total):
    for part in range(2):
        count = received[0].shape[1] // 2
        rows_high, rows_low = split_halves(table_rows(near, far, first, share, blocks, part))
        coefs = jnp.concatenate(
            [other[:, part * count : (part + 1) * count] for other in received], axis=0
        )
        term = dot_columns(coefs, rows_high) + dot_columns(coefs, rows_low)
        total = term if total is None else total + term
    return total


VMEM = pl.BlockSpec(memory_space=pltpu.VMEM)
SMEM = pl.BlockSpec(memory_space=pltpu.SMEM)
HBM = pl.BlockSpec(memory_space=pltpu.HBM)


def grant(size):
    return pltpu.CompilerParams(vmem_limit_bytes=size << 20)


def cost(microseconds):
    return pl.CostEstimate(flops=0, bytes_accessed=int(microseconds * 3.3e6), transcendentals=0)


def like(shape, dtype):
    return jax.ShapeDtypeStruct(shape, dtype)


def whole_block(shape):
    return pl.BlockSpec(shape, lambda *_: (0,) * len(shape))


def shards(
    level_fields, wind_field, zonal_step, quad_weight, legendre, wave_table, damping, vertical
):
    levels, hemis, rows_half, lon_dev = level_fields.shape
    slots_dev, _, columns = legendre.shape
    lat_count = lax.axis_size("lat")
    lon_count = lax.axis_size("lon")
    degree_dev = columns // lat_count
    if (
        rows_half % 16
        or degree_dev % 16
        or lon_dev % LANES
        or slots_dev != sum(CUTS)
        or levels != 2
        or lat_count & (lat_count - 1)
        or lat_count < 4
        or lon_count & (lon_count - 1)
        or lon_count < 4
    ):
        return untiled(
            level_fields,
            wind_field,
            zonal_step,
            quad_weight,
            legendre,
            wave_table,
            damping,
            vertical,
        )
    lat_index = lax.axis_index("lat")
    lon_index = lax.axis_index("lon")
    planes = levels * hemis
    grid_count = planes * rows_half
    sections = 2 * planes
    half = sections // 2
    width = 2 * grid_count
    fields = level_fields.reshape(planes, rows_half, lon_dev)
    winds = wind_field.reshape(2 * hemis, rows_half, lon_dev)

    fields, winds, first_row, last_row, first_column, last_column = pl.pallas_call(
        load_kernel,
        out_shape=[pltpu.VMEM(fields.shape, F32), pltpu.VMEM(winds.shape, F32)]
        + [like((planes, lon_dev), F32)] * 2
        + [like((rows_half, planes), F32)] * 2,
        in_specs=[HBM] * 2,
        out_specs=[VMEM] * 6,
        scratch_shapes=[pltpu.SemaphoreType.DMA((2,))],
        compiler_params=grant(8),
        cost_estimate=cost(1.5),
        name="load",
    )(*[pltpu.with_memory_space_constraint(value, pltpu.HBM) for value in (fields, winds)])
    up = [(i, (i + 1) % lat_count) for i in range(lat_count)]
    east = [(i, (i + 1) % lon_count) for i in range(lon_count)]
    down = [(j, i) for i, j in up]
    west = [(j, i) for i, j in east]
    above = lax.ppermute(last_row, "lat", up)
    below = lax.ppermute(first_row, "lat", down)
    before = lax.ppermute(last_column, "lon", east)
    after = lax.ppermute(first_column, "lon", west)

    order = [
        lax.dynamic_slice_in_dim(wave_table, (lon_index ^ k) * slots_dev, slots_dev)
        for k in range(lon_count)
    ]
    my_waves = order[0]
    waves = jnp.concatenate(order)
    near_angle = angle_table(waves, jnp.arange(LANES, dtype=jnp.int32))
    near = jnp.concatenate([jnp.cos(near_angle), jnp.sin(near_angle)], axis=1)
    far_angle = angle_table(
        waves, lon_index * lon_dev + LANES * jnp.arange(lon_dev // LANES, dtype=jnp.int32)
    )
    far = jnp.concatenate([jnp.cos(far_angle), jnp.sin(far_angle)], axis=1) / math.sqrt(NLON)

    flags = jnp.stack([lat_index == 0, lat_index == lat_count - 1]).astype(jnp.int32)
    place = lat_index.astype(jnp.int32).reshape(1)
    weight_row = jnp.tile(quad_weight, sections)[None, :]

    def sums_shape(share):
        return [like((lon_count // 2, share, width), dtype) for dtype in (F32, BF16)]

    def first_sums(flags_ref, fields_ref, winds_ref, step_ref, *refs):
        edges, near_ref, far_ref, stepped_ref = refs[:4], refs[4], refs[5], refs[6]
        advance(flags_ref, fields_ref, winds_ref, step_ref, *edges, stepped_ref)
        zonal_sums(lon_count, CUTS[0], 0, stepped_ref, near_ref, far_ref, refs[7:])

    stepped, *pieces = pl.pallas_call(
        first_sums,
        out_shape=[like((grid_count, lon_dev), F32)] + sums_shape(CUTS[0]),
        in_specs=[SMEM] + [VMEM] * 9,
        out_specs=[VMEM] * 3,
        compiler_params=grant(24),
        cost_estimate=cost(3.0),
        name="advance_and_sums",
    )(flags, fields, winds, zonal_step[None, :], above, below, before, after, near, far)

    def later_sums(share, first, after):
        def body(stepped_ref, near_ref, far_ref, after_ref, *outs):
            zonal_sums(lon_count, share, first, stepped_ref, near_ref, far_ref, outs)

        return pl.pallas_call(
            body,
            out_shape=sums_shape(share),
            in_specs=[VMEM] * 4,
            out_specs=[VMEM] * 2,
            compiler_params=grant(24),
            cost_estimate=cost(0.025 * share),
            name="sums",
        )(stepped, near, far, after)

    def to_owners(own, pair):
        pair = lax.ppermute(pair, "lon", pairs(lon_count, 1))
        parts = [own[0], pair[0]]
        for k in range(1, lon_count // 2):
            joint = (own[k] + pair[k].astype(F32)).astype(BF16)
            parts.append(lax.ppermute(joint, "lon", pairs(lon_count, 2 * k)))
        return parts

    def from_owners(coefs):
        near_by = lax.ppermute(coefs, "lon", pairs(lon_count, 1))
        parts = [coefs, near_by]
        for k in range(1, lon_count // 2):
            distant = lax.ppermute(coefs, "lon", pairs(lon_count, 2 * k))
            parts += [distant, lax.ppermute(distant, "lon", pairs(lon_count, 1))]
        return parts

    swapped, first = [to_owners(*pieces)], CUTS[0]
    for share in CUTS[1:]:
        pieces = later_sums(share, first, pieces[0])
        swapped.append(to_owners(*pieces))
        first += share
    table = pl.pallas_call(
        load_table_kernel,
        out_shape=pltpu.VMEM(legendre.shape, BF16),
        in_specs=[VMEM, HBM],
        out_specs=VMEM,
        scratch_shapes=[pltpu.SemaphoreType.DMA((4,))],
        compiler_params=grant(8),
        cost_estimate=cost(5.7),
        name="load_table",
    )(pieces[0], pltpu.with_memory_space_constraint(legendre, pltpu.HBM))

    def forward(first, share, parts, earlier, last):
        if last:
            shape = (lat_count // 2, degree_dev, half * slots_dev)
            shapes = [like(shape, F32)] * 2
        else:
            shapes = [like((columns, half * share), F32)]
        return pl.pallas_call(
            lambda *refs: forward_kernel(
                len(parts), sections, rows_half, degree_dev, first, last, *refs
            ),
            out_shape=shapes,
            grid_spec=pltpu.PrefetchScalarGridSpec(
                num_scalar_prefetch=2,
                grid=(share // GROUP,),
                in_specs=[whole_block((share, width))] * len(parts)
                + [whole_block((1, width)), VMEM]
                + [whole_block(other.shape) for other in earlier],
                out_specs=[whole_block(shape.shape) for shape in shapes],
                scratch_shapes=[
                    pltpu.VMEM((share, sections, LANES), F32),
                    pltpu.VMEM((columns // LANES, half * share, LANES), F32),
                    pltpu.VMEM((columns, half * share), F32),
                ],
            ),
            compiler_params=grant(20),
            cost_estimate=cost(0.05 * share + 0.7),
            name="forward",
        )(my_waves[first : first + share], place, *parts, weight_row, table, *earlier)

    earlier, first = [], 0
    for share, parts in zip(CUTS, swapped):
        last = first + share == slots_dev
        earlier = earlier + list(forward(first, share, parts, earlier, last))
        first += share
    own, other = earlier[-2:]

    other = lax.ppermute(other, "lat", pairs(lat_count, 1))
    sums = [own[j] + other[j] for j in range(lat_count // 2)]
    sums = [sums[0]] + [
        lax.ppermute(sums[j].astype(BF16), "lat", pairs(lat_count, 2 * j))
        for j in range(1, lat_count // 2)
    ]
    rounded, spectrum = pl.pallas_call(
        lambda *refs: correct_kernel(CUTS, levels, *refs),
        out_shape=[
            like((degree_dev, half * slots_dev), BF16),
            like((half, degree_dev, slots_dev), F32),
        ],
        in_specs=[SMEM] * 3 + [VMEM] * len(sums),
        out_specs=[VMEM] * 2,
        compiler_params=grant(8),
        name="correct",
    )(place, damping, vertical, *sums)
    joined = lax.all_gather(rounded, "lat", axis=0, tiled=True)

    def inverse(first, share, after):
        count = 3 + len(after)
        return pl.pallas_call(
            lambda *refs: inverse_kernel(sections, rows_half, first, *refs[:3], *refs[count:]),
            out_shape=like((share, width), BF16),
            grid_spec=pltpu.PrefetchScalarGridSpec(
                num_scalar_prefetch=1,
                grid=(share // GROUP,),
                in_specs=[whole_block(joined.shape), VMEM] + [VMEM] * len(after),
                out_specs=whole_block((share, width)),
                scratch_shapes=[
                    pltpu.VMEM((columns // LANES, half * share, LANES), F32),
                    pltpu.VMEM((share, sections, LANES), F32),
                ],
            ),
            compiler_params=grant(20),
            cost_estimate=cost(0.06 * share + 0.3),
            name="inverse",
        )(my_waves[first : first + share], joined, table, *after)

    def values(first, share, parts, base):
        def body(near_ref, far_ref, *refs):
            start = refs[lon_count][...] if base else None
            refs[-1][...] = zonal_values(
                lon_count, share, first, near_ref, far_ref, refs[:lon_count], start
            )

        return pl.pallas_call(
            body,
            out_shape=like((grid_count, lon_dev), F32),
            in_specs=[VMEM] * (2 + lon_count + len(base)),
            out_specs=VMEM,
            compiler_params=grant(24),
            cost_estimate=cost(0.025 * share),
            name="values",
        )(near, far, *parts, *base)

    base, first, coefs = [], slots_dev, []
    for share in reversed(CUTS):
        first -= share
        coefs = [inverse(first, share, coefs)]
        base = [values(first, share, from_owners(coefs[0]), base)]
    spectrum = spectrum.reshape(2, levels, degree_dev, slots_dev).transpose(2, 3, 0, 1)
    return (base[0].reshape(level_fields.shape), spectrum)


def solution(mesh):
    return jax.shard_map(
        shards,
        mesh=mesh,
        in_specs=(
            P(None, None, "lat", "lon"),
            P(None, None, "lat", "lon"),
            P("lat"),
            P("lat"),
            P("lon", "lat", None),
            P(),
            P(),
            P(),
        ),
        out_specs=(P(None, None, "lat", "lon"), P("lat", "lon", None, None)),
        check_vma=False,
    )
```

```python
import math

import jax
import jax.numpy as jnp
from jax import lax
from jax.experimental import pallas as pl
from jax.experimental.pallas import tpu as pltpu
from jax.sharding import PartitionSpec as P


NLON = 2560
M = 640


HIGHEST_PRECISION = lax.Precision.HIGHEST


def padded(cells, sides, width):
    for axis, dim in sides:
        count = lax.axis_size(axis)
        head = lax.slice_in_dim(cells, 0, width, axis=dim)
        tail = lax.slice_in_dim(cells, cells.shape[dim] - width, cells.shape[dim], axis=dim)
        cells = jnp.concatenate(
            [
                lax.ppermute(tail, axis, [(i, (i + 1) % count) for i in range(count)]),
                cells,
                lax.ppermute(head, axis, [((i + 1) % count, i) for i in range(count)]),
            ],
            axis=dim,
        )
    return cells


def angle_table(waves, columns):
    return (waves[:, None] * columns[None, :] % NLON).astype(jnp.float32) * (2.0 * math.pi / NLON)


def correct(spectrum, degrees, damping, vertical):
    modal = jnp.einsum("kl,nmcl->nmck", vertical, spectrum, precision=HIGHEST_PRECISION)
    divisor = 1.0 + damping[None, :] * (degrees * (degrees + 1)).astype(jnp.float32)[
        :, None
    ] / float(M * M)
    modal = modal / divisor[:, None, None, :]
    return jnp.einsum("kl,nmck->nmcl", vertical, modal, precision=HIGHEST_PRECISION)


def untiled(
    level_fields, wind_field, zonal_step, quad_weight, legendre, wave_table, damping, vertical
):
    levels, hemis, rows_half, lon_dev = level_fields.shape
    slots_dev = legendre.shape[0]
    lat_count = lax.axis_size("lat")
    lat_index = lax.axis_index("lat")
    lon_index = lax.axis_index("lon")
    degree_dev = M // lat_count
    grid_count = levels * hemis * rows_half
    contract_last = (((1,), (1,)), ((), ()))
    contract_first = (((0,), (0,)), ((), ()))
    batch_slots = (((2,), (1,)), ((0,), (0,)))
    extended = padded(level_fields, (("lat", 2), ("lon", 3)), 1)
    eastward = extended[:, :, 1:-1, 2:]
    westward = extended[:, :, 1:-1, :-2]
    toward = extended[:, :, 2:, 1:-1]
    poleward = extended[:, :, :-2, 1:-1]
    row_number = jnp.arange(rows_half)
    at_equator = (row_number == rows_half - 1) & (lat_index == lat_count - 1)
    toward = jnp.where(at_equator[:, None], level_fields[:, ::-1, -1:, :], toward)
    at_pole = (row_number == 0) & (lat_index == 0)
    poleward = jnp.where(at_pole[:, None], 0.0, poleward)
    tendency = wind_field[0] * zonal_step[:, None] * (eastward - westward) + 0.25 * wind_field[
        1
    ] * (toward - poleward)
    stepped = level_fields - tendency
    my_waves = lax.dynamic_slice_in_dim(wave_table, lon_index * slots_dev, slots_dev)
    portion = lax.all_gather(stepped, "lon", axis=3, tiled=True)
    lon_width = portion.shape[3]
    columns = jnp.arange(lon_width, dtype=jnp.int32)
    angles = angle_table(my_waves, columns)
    values = portion.reshape(grid_count, lon_width)
    cosine_sum = lax.dot_general(
        jnp.cos(angles), values, contract_last, precision=HIGHEST_PRECISION
    )
    sine_sum = lax.dot_general(jnp.sin(angles), values, contract_last, precision=HIGHEST_PRECISION)
    cosine_sum, sine_sum = (cosine_sum, sine_sum)
    fourier = jnp.stack([cosine_sum, -sine_sum], axis=1) / math.sqrt(NLON)
    weighted = (fourier.reshape(slots_dev, 2, levels, hemis, rows_half) * quad_weight).astype(
        jnp.bfloat16
    )
    weighted = weighted.reshape(slots_dev, 2 * levels * hemis, rows_half)
    table_part = legendre
    summed = lax.dot_general(weighted, table_part, batch_slots, preferred_element_type=jnp.float32)
    summed = summed.reshape(slots_dev, 2, levels, hemis, degree_dev * lax.axis_size("lat"))
    degrees = jnp.arange(degree_dev * lax.axis_size("lat"), dtype=jnp.int32)
    parity = jnp.where((degrees[None, :] - my_waves[:, None]) % 2 == 0, 1.0, -1.0)
    kept_mask = degrees[None, :] >= my_waves[:, None]
    combined = summed[:, :, :, 0] + parity[:, None, None, :] * summed[:, :, :, 1]
    combined = jnp.where(kept_mask[:, None, None, :], combined, 0.0)
    raw = lax.psum_scatter(combined.transpose(3, 0, 1, 2), "lat", scatter_dimension=0, tiled=True)
    my_degrees = lat_index * degree_dev + jnp.arange(degree_dev, dtype=jnp.int32)
    spectrum = correct(raw, my_degrees, damping, vertical)
    portion = lax.all_gather(spectrum.astype(jnp.bfloat16), "lat", axis=0, tiled=True)
    row_count = portion.shape[0]
    table_part = legendre
    degrees = jnp.arange(row_count, dtype=jnp.int32)
    even_mask = ((degrees[None, :] - my_waves[:, None]) % 2 == 0)[:, :, None]
    arranged = portion.transpose(1, 0, 2, 3).reshape(slots_dev, row_count, 2 * levels)
    even_sum = lax.dot_general(
        table_part,
        jnp.where(even_mask, arranged, 0),
        batch_slots,
        preferred_element_type=jnp.float32,
    )
    odd_sum = lax.dot_general(
        table_part,
        jnp.where(even_mask, 0, arranged),
        batch_slots,
        preferred_element_type=jnp.float32,
    )
    even_sum, odd_sum = (even_sum, odd_sum)
    coefs = jnp.stack([even_sum + odd_sum, even_sum - odd_sum], axis=1) / math.sqrt(M)
    coefs = (
        coefs.reshape(slots_dev, 2, rows_half, 2, levels)
        .transpose(0, 3, 4, 1, 2)
        .reshape(slots_dev, 2, grid_count)
    )
    my_columns = lon_index * lon_dev + jnp.arange(lon_dev, dtype=jnp.int32)
    portion = lax.all_gather(coefs, "lon", axis=0, tiled=True)
    factor = jnp.where(wave_table == 0, 1.0, 2.0)[:, None]
    angles = angle_table(wave_table, my_columns)
    totals = lax.dot_general(
        portion[:, 0], jnp.cos(angles) * factor, contract_first, precision=HIGHEST_PRECISION
    )
    grid_out = totals - lax.dot_general(
        portion[:, 1], jnp.sin(angles) * factor, contract_first, precision=HIGHEST_PRECISION
    )
    new_fields = (grid_out / math.sqrt(NLON)).reshape(level_fields.shape)
    return (new_fields, spectrum)


CUTS = (64, 64, 32)
GROUP = 16
LANES = 128
F32 = jnp.float32
BF16 = jnp.bfloat16


def split_halves(value):
    high = value.astype(BF16)
    return high, (value - high.astype(F32)).astype(BF16)


def dot_rows(left, right):
    return lax.dot_general(left, right, (((1,), (1,)), ((), ())), preferred_element_type=F32)


def dot_columns(left, right):
    return lax.dot_general(left, right, (((0,), (0,)), ((), ())), preferred_element_type=F32)


def pairs(count, step):
    return [(i, i ^ step) for i in range(count)]


def load_kernel(fields_hbm, winds_hbm, fields_ref, winds_ref, *refs):
    first_row, last_row, first_column, last_column, semaphores = refs
    fields_copy = pltpu.make_async_copy(fields_hbm, fields_ref, semaphores.at[0])
    winds_copy = pltpu.make_async_copy(winds_hbm, winds_ref, semaphores.at[1])
    fields_copy.start()
    winds_copy.start()
    fields_copy.wait()
    count, rows, columns = fields_ref.shape
    for p in range(count):
        first_row[p : p + 1, :] = fields_ref[p, 0:1, :]
        last_row[p : p + 1, :] = fields_ref[p, rows - 1 : rows, :]
        first_column[:, p : p + 1] = fields_ref[p, :, 0:1]
        last_column[:, p : p + 1] = fields_ref[p, :, columns - 1 : columns]
    winds_copy.wait()


def table_copy(table_hbm, table_ref, first, step, semaphores):
    at = pl.multiple_of(step * GROUP, GROUP)
    return pltpu.make_async_copy(
        table_hbm.at[pl.ds(first + at, GROUP)],
        table_ref.at[pl.ds(at, GROUP)],
        semaphores.at[step],
    )


def advance(flags, fields_ref, wind_ref, step_ref, above, below, before, after, stepped_ref):
    count, rows, columns = fields_ref.shape
    lane = lax.broadcasted_iota(jnp.int32, (rows, columns), 1)
    row = lax.broadcasted_iota(jnp.int32, (rows, columns), 0)
    square = (rows, rows)
    diagonal = lax.broadcasted_iota(jnp.int32, square, 0) == lax.broadcasted_iota(
        jnp.int32, square, 1
    )
    steps = jnp.sum(jnp.where(diagonal, step_ref[...], 0.0), axis=1, keepdims=True)
    for p in range(count):
        h = p % 2
        field = fields_ref[p]
        eastward = jnp.where(
            lane == columns - 1, after[:, p : p + 1], pltpu.roll(field, columns - 1, 1)
        )
        westward = jnp.where(lane == 0, before[:, p : p + 1], pltpu.roll(field, 1, 1))
        other = fields_ref[p ^ 1, rows - 1 : rows, :]
        low_edge = jnp.where(flags[1] == 1, other, below[p : p + 1, :])
        high_edge = jnp.where(flags[0] == 1, 0.0, above[p : p + 1, :])
        toward = jnp.where(row == rows - 1, low_edge, pltpu.roll(field, rows - 1, 0))
        poleward = jnp.where(row == 0, high_edge, pltpu.roll(field, 1, 0))
        tendency = wind_ref[h] * steps * (eastward - westward) + 0.25 * wind_ref[
            2 + h
        ] * (toward - poleward)
        stepped_ref[p * rows : (p + 1) * rows, :] = field - tendency


def table_rows(near, far, first, share, blocks, part):
    per_block = near.shape[0] // blocks
    half = far.shape[1] // 2
    out = []
    for k in range(blocks):
        at = pl.ds(k * per_block + first, share)
        near_cos, near_sin = near[at, :LANES], near[at, LANES:]
        far_cos, far_sin = far[at, :half], far[at, half:]
        columns = []
        for j in range(half):
            c, s = far_cos[:, j : j + 1], far_sin[:, j : j + 1]
            if part:
                columns.append(-(s * near_cos + c * near_sin))
            else:
                columns.append(c * near_cos - s * near_sin)
        out.append(jnp.concatenate(columns, axis=1))
    return jnp.concatenate(out, axis=0)


def zonal_sums(blocks, share, first, stepped_ref, near, far, outs):
    high, low = split_halves(stepped_ref[...])
    count = stepped_ref.shape[0]
    for part in range(2):
        rows_high, rows_low = split_halves(table_rows(near, far, first, share, blocks, part))
        sums = dot_rows(rows_high, high) + (dot_rows(rows_high, low) + dot_rows(rows_low, high))
        lanes = slice(part * count, (part + 1) * count)
        own, pair = outs
        for k in range(0, blocks, 2):
            own[k // 2, :, lanes] = sums[k * share : (k + 1) * share, :]
            pair[k // 2, :, lanes] = sums[(k + 1) * share : (k + 2) * share, :].astype(BF16)


def forward_kernel(
    blocks, sections, rows, degree_dev, first, last, waves_ref, place_ref, *refs
):
    received = refs[:blocks]
    weight_ref, table_hbm = refs[blocks : blocks + 2]
    *rest, table_ref, semaphores = refs[blocks + 2 :]
    spread_ref, kept_ref, turned_ref = rest[-3:]
    step = pl.program_id(0)
    half = sections // 2
    levels = half // 2
    group = GROUP
    columns = table_ref.shape[2]
    share = spread_ref.shape[0]

    @pl.when(step == 0)
    def _():
        for i in range(share // group):
            table_copy(table_hbm, table_ref, first, i, semaphores).start()
        total = received[0][...].astype(F32)
        for other in received[1:]:
            total = total + other[...].astype(F32)
        total = total * weight_ref[...]
        for c in range(2):
            for level in range(levels):
                for h in range(2):
                    at = ((c * levels + level) * 2 + h) * rows
                    spread_ref[:, h * half + level * 2 + c, 0:rows] = total[:, at : at + rows]

    table_copy(table_hbm, table_ref, first, step, semaphores).wait()
    degree = lax.broadcasted_iota(jnp.int32, (2 * half, columns), 1)
    row = lax.broadcasted_iota(jnp.int32, (2 * half, 1), 0)
    for u in range(0, group, 2):
        sums = []
        for v in (u, u + 1):
            high, low = split_halves(spread_ref[step * group + v, :, 0:rows])
            both = jnp.concatenate([high.astype(F32), low.astype(F32)], axis=0).astype(BF16)
            total = jnp.dot(both, table_ref[step * group + v], preferred_element_type=F32)
            sums.append(total[:sections] + total[sections:])
        north = jnp.concatenate([sums[0][:half], sums[1][:half]], axis=0)
        south = jnp.concatenate([sums[0][half:], sums[1][half:]], axis=0)
        slot = step * group + u
        past = degree - jnp.where(row < half, waves_ref[slot], waves_ref[slot + 1])
        combined = north + jnp.where(past & 1 == 0, south, -south)
        combined = jnp.where(past >= 0, combined, 0.0)
        at = pl.ds(pl.multiple_of(slot * half, 2 * half), 2 * half)
        for t in range(columns // LANES):
            kept_ref[t, at, :] = combined[:, t * LANES : (t + 1) * LANES]

    @pl.when(step == pl.num_programs(0) - 1)
    def _():
        target = turned_ref if last else rest[-4]
        for t in range(columns // LANES):
            tile = jnp.concatenate(
                [kept_ref[t, pl.ds(j, share, stride=half), :] for j in range(half)], axis=0
            )
            target[t * LANES : (t + 1) * LANES, :] = tile.T
        if not last:
            return
        earlier, (own_ref, other_ref) = rest[:-5], rest[-5:-3]
        for j in range(own_ref.shape[0]):
            for out, k in ((own_ref, 2 * j), (other_ref, 2 * j + 1)):
                at = pl.ds(pl.multiple_of((place_ref[0] ^ k) * degree_dev, 8), degree_dev)
                done = 0
                for source in (*earlier, turned_ref):
                    wide = source.shape[1]
                    out[j, :, done : done + wide] = source[at, :]
                    done += wide


def correct_kernel(
    cuts, levels, place_ref, damping_ref, vertical_ref, sum_ref, *refs
):
    others, (rounded_ref, spectrum_ref) = refs[:-2], refs[-2:]
    total = sum_ref[...]
    for other in others:
        total = total + other[...].astype(F32)
    count = total.shape[0]
    degree = place_ref[0] * count + lax.broadcasted_iota(jnp.int32, (count, 1), 0)
    growth = (degree * (degree + 1)).astype(F32) / float(M * M)
    scale = [1.0 / (1.0 + damping_ref[k] * growth) for k in range(levels)]
    at, slot = 0, 0
    for share in cuts:
        wide = 2 * share
        raw = [total[:, at + l * wide : at + (l + 1) * wide] for l in range(levels)]
        modal = [
            sum(vertical_ref[k, l] * raw[l] for l in range(levels)) * scale[k]
            for k in range(levels)
        ]
        for l in range(levels):
            value = sum(vertical_ref[k, l] * modal[k] for k in range(levels))
            rounded_ref[:, at + l * wide : at + (l + 1) * wide] = value.astype(BF16)
            for c in range(2):
                spectrum_ref[c * levels + l, :, slot : slot + share] = value[
                    :, c * share : (c + 1) * share
                ]
        at, slot = at + levels * wide, slot + share


def inverse_kernel(sections, rows, first, waves_ref, joined_ref, table_hbm, *refs):
    own_ref, out_ref, kept_ref, spread_ref, table_ref, semaphores = refs
    step = pl.program_id(0)
    half = sections // 2
    levels = half // 2
    group = GROUP
    columns = table_ref.shape[2]
    share = spread_ref.shape[0]

    @pl.when(step == 0)
    def _():
        for i in range(share // group):
            table_copy(table_hbm, table_ref, first, i, semaphores).start()
        for t in range(columns // LANES):
            tile = joined_ref[t * LANES : (t + 1) * LANES, half * first : half * (first + share)]
            turned = tile.astype(F32).T
            for j in range(half):
                kept_ref[t, pl.ds(j, share, stride=half), :] = turned[
                    j * share : (j + 1) * share, :
                ]

    degree = lax.broadcasted_iota(jnp.int32, (2 * half, columns), 1)
    row = lax.broadcasted_iota(jnp.int32, (2 * half, 1), 0)
    upper = row < half
    table_copy(table_hbm, table_ref, first, step, semaphores).wait()
    for u in range(0, group, 2):
        slot = step * group + u
        at = pl.ds(pl.multiple_of(slot * half, 2 * half), 2 * half)
        values = jnp.concatenate(
            [kept_ref[t, at, :] for t in range(columns // LANES)], axis=1
        )
        even = (degree - jnp.where(upper, waves_ref[slot], waves_ref[slot + 1])) & 1 == 0
        evens = jnp.where(even, values, 0.0)
        odds = pltpu.roll(jnp.where(even, 0.0, values), half, 0)
        for v in range(2):
            both = jnp.where(upper, odds, evens) if v else jnp.where(upper, evens, odds)
            sums = dot_rows(both.astype(BF16), table_ref[slot + v])
            factor = jnp.where(waves_ref[slot + v] == 0, 1.0, 2.0) / math.sqrt(M)
            sums = sums * factor
            swapped = pltpu.roll(sums, half, 0)
            less = sums - swapped if v else swapped - sums
            spread_ref[slot + v, :, 0:rows] = jnp.where(upper, sums + swapped, less)

    @pl.when(step == pl.num_programs(0) - 1)
    def _():
        for c in range(2):
            for level in range(levels):
                for h in range(2):
                    at = ((c * levels + level) * 2 + h) * rows
                    value = spread_ref[:, h * half + level * 2 + c, 0:rows]
                    own_ref[:, at : at + rows] = value
                    out_ref[:, at : at + rows] = value.astype(out_ref.dtype)


def zonal_values(blocks, share, first, near, far, received, total):
    for part in range(2):
        count = received[0].shape[1] // 2
        rows_high, rows_low = split_halves(table_rows(near, far, first, share, blocks, part))
        lanes = slice(part * count, (part + 1) * count)
        own_high, own_low = split_halves(received[0][:, lanes])
        coefs = jnp.concatenate([own_high] + [other[:, lanes] for other in received[1:]], axis=0)
        term = dot_columns(coefs, rows_high) + dot_columns(coefs, rows_low)
        term = term + dot_columns(own_low, rows_high[:share])
        total = term if total is None else total + term
    return total


VMEM = pl.BlockSpec(memory_space=pltpu.VMEM)
SMEM = pl.BlockSpec(memory_space=pltpu.SMEM)
HBM = pl.BlockSpec(memory_space=pltpu.HBM)


def grant(size):
    return pltpu.CompilerParams(vmem_limit_bytes=size << 20)


def cost(microseconds):
    return pl.CostEstimate(flops=0, bytes_accessed=int(microseconds * 3.3e6), transcendentals=0)


def like(shape, dtype):
    return jax.ShapeDtypeStruct(shape, dtype)


def whole_block(shape):
    return pl.BlockSpec(shape, lambda *_: (0,) * len(shape))


def tiled(
    level_fields, wind_field, zonal_step, quad_weight, legendre, wave_table, damping, vertical
):
    levels, hemis, rows_half, lon_dev = level_fields.shape
    slots_dev, _, columns = legendre.shape
    lat_count = lax.axis_size("lat")
    lon_count = lax.axis_size("lon")
    degree_dev = columns // lat_count
    lat_index = lax.axis_index("lat")
    lon_index = lax.axis_index("lon")
    planes = levels * hemis
    grid_count = planes * rows_half
    sections = 2 * planes
    half = sections // 2
    width = 2 * grid_count
    fields = level_fields.reshape(planes, rows_half, lon_dev)
    winds = wind_field.reshape(2 * hemis, rows_half, lon_dev)

    fields, winds, first_row, last_row, first_column, last_column = pl.pallas_call(
        load_kernel,
        out_shape=[pltpu.VMEM(fields.shape, F32), pltpu.VMEM(winds.shape, F32)]
        + [like((planes, lon_dev), F32)] * 2
        + [like((rows_half, planes), F32)] * 2,
        in_specs=[HBM] * 2,
        out_specs=[VMEM] * 6,
        scratch_shapes=[pltpu.SemaphoreType.DMA((2,))],
        compiler_params=grant(8),
        cost_estimate=cost(1.5),
        name="load",
    )(*[pltpu.with_memory_space_constraint(value, pltpu.HBM) for value in (fields, winds)])
    up = [(i, (i + 1) % lat_count) for i in range(lat_count)]
    east = [(i, (i + 1) % lon_count) for i in range(lon_count)]
    down = [(j, i) for i, j in up]
    west = [(j, i) for i, j in east]
    above = lax.ppermute(last_row, "lat", up)
    below = lax.ppermute(first_row, "lat", down)
    before = lax.ppermute(last_column, "lon", east)
    after = lax.ppermute(first_column, "lon", west)

    order = [
        lax.dynamic_slice_in_dim(wave_table, (lon_index ^ k) * slots_dev, slots_dev)
        for k in range(lon_count)
    ]
    my_waves = order[0]
    waves = jnp.concatenate(order)
    near_angle = angle_table(waves, jnp.arange(LANES, dtype=jnp.int32))
    near = jnp.concatenate([jnp.cos(near_angle), jnp.sin(near_angle)], axis=1)
    far_angle = angle_table(
        waves, lon_index * lon_dev + LANES * jnp.arange(lon_dev // LANES, dtype=jnp.int32)
    )
    far = jnp.concatenate([jnp.cos(far_angle), jnp.sin(far_angle)], axis=1) / math.sqrt(NLON)

    flags = jnp.stack([lat_index == 0, lat_index == lat_count - 1]).astype(jnp.int32)
    place = lat_index.astype(jnp.int32).reshape(1)
    weight_row = jnp.tile(quad_weight, sections)[None, :]

    def sums_shape(share):
        return [like((lon_count // 2, share, width), dtype) for dtype in (F32, BF16)]

    table = pltpu.with_memory_space_constraint(legendre, pltpu.HBM)

    def first_sums(flags_ref, fields_ref, winds_ref, step_ref, *refs):
        edges, near_ref, far_ref, stepped_ref = refs[:4], *refs[4:7]
        advance(flags_ref, fields_ref, winds_ref, step_ref, *edges, stepped_ref)
        zonal_sums(lon_count, CUTS[0], 0, stepped_ref, near_ref, far_ref, refs[7:])

    stepped, *pieces = pl.pallas_call(
        first_sums,
        out_shape=[like((grid_count, lon_dev), F32)] + sums_shape(CUTS[0]),
        in_specs=[SMEM] + [VMEM] * 9,
        out_specs=[VMEM] * 3,
        compiler_params=grant(20),
        cost_estimate=cost(3.0),
        name="advance_and_sums",
    )(
        flags, fields, winds, zonal_step[None, :], above, below, before, after, near, far
    )

    def later_sums(chunk, first, after):
        share = CUTS[chunk]

        def body(stepped_ref, near_ref, far_ref, after_ref, *outs):
            zonal_sums(lon_count, share, first, stepped_ref, near_ref, far_ref, outs)

        return pl.pallas_call(
            body,
            out_shape=sums_shape(share),
            in_specs=[VMEM] * 4,
            out_specs=[VMEM] * 2,
            compiler_params=grant(20),
            cost_estimate=cost(0.035 * share),
            name="sums",
        )(stepped, near, far, after)

    def swap(value, axis, step):
        return lax.ppermute(value, axis, pairs(lax.axis_size(axis), step))

    def to_owners(own, pair):
        pair = swap(pair, "lon", 1)
        parts = [own[0], pair[0]]
        for k in range(1, lon_count // 2):
            joint = (own[k] + pair[k].astype(F32)).astype(BF16)
            parts.append(swap(joint, "lon", 2 * k))
        return parts

    def from_owners(own, coefs):
        parts = [own, swap(coefs, "lon", 1)]
        for k in range(1, lon_count // 2):
            distant = swap(coefs, "lon", 2 * k)
            parts += [distant, swap(distant, "lon", 1)]
        return parts

    swapped, first = [to_owners(*pieces)], CUTS[0]
    for chunk in range(1, len(CUTS)):
        pieces = later_sums(chunk, first, pieces[0])
        swapped.append(to_owners(*pieces))
        first += CUTS[chunk]


    def forward(first, share, parts, earlier, last):
        if last:
            shape = (lat_count // 2, degree_dev, half * slots_dev)
            shapes = [like(shape, F32)] * 2
        else:
            shapes = [like((columns, half * share), F32)]
        return pl.pallas_call(
            lambda *refs: forward_kernel(
                len(parts), sections, rows_half, degree_dev, first, last, *refs
            ),
            out_shape=shapes,
            grid_spec=pltpu.PrefetchScalarGridSpec(
                num_scalar_prefetch=2,
                grid=(share // GROUP,),
                in_specs=[whole_block((share, width))] * len(parts)
                + [whole_block((1, width)), HBM]
                + [whole_block(other.shape) for other in earlier],
                out_specs=[whole_block(shape.shape) for shape in shapes],
                scratch_shapes=[
                    pltpu.VMEM((share, sections, LANES), F32),
                    pltpu.VMEM((columns // LANES, half * share, LANES), F32),
                    pltpu.VMEM((columns, half * share), F32),
                    pltpu.VMEM((share, rows_half, columns), BF16),
                    pltpu.SemaphoreType.DMA((share // GROUP,)),
                ],
            ),
            compiler_params=grant(20),
            cost_estimate=cost(0.05 * share + 0.7),
            name="forward",
        )(my_waves[first : first + share], place, *parts, weight_row, table, *earlier)

    earlier, first = [], 0
    for chunk, share in enumerate(CUTS):
        last = chunk == len(CUTS) - 1
        earlier += forward(first, share, swapped[chunk], earlier, last)
        first += share
    own, other = earlier[-2:]

    other = swap(other, "lat", 1)
    sums = [own[j] + other[j] for j in range(lat_count // 2)]
    sums = [sums[0]] + [swap(sums[j], "lat", 2 * j) for j in range(1, lat_count // 2)]
    rounded, spectrum = pl.pallas_call(
        lambda *refs: correct_kernel(CUTS, levels, *refs),
        out_shape=[
            like((degree_dev, half * slots_dev), BF16),
            like((half, degree_dev, slots_dev), F32),
        ],
        in_specs=[SMEM] * 3 + [VMEM] * len(sums),
        out_specs=[VMEM] * 2,
        compiler_params=grant(8),
        name="correct",
    )(place, damping, vertical, *sums)
    joined = lax.all_gather(rounded, "lat", axis=0, tiled=True)

    def inverse(first, share, after):
        count = 3 + len(after)
        return pl.pallas_call(
            lambda *refs: inverse_kernel(sections, rows_half, first, *refs[:3], *refs[count:]),
            out_shape=[like((share, width), F32), like((share, width), BF16)],
            grid_spec=pltpu.PrefetchScalarGridSpec(
                num_scalar_prefetch=1,
                grid=(share // GROUP,),
                in_specs=[whole_block(joined.shape), HBM] + [VMEM] * len(after),
                out_specs=[whole_block((share, width))] * 2,
                scratch_shapes=[
                    pltpu.VMEM((columns // LANES, half * share, LANES), F32),
                    pltpu.VMEM((share, sections, LANES), F32),
                    pltpu.VMEM((share, rows_half, columns), BF16),
                    pltpu.SemaphoreType.DMA((share // GROUP,)),
                ],
            ),
            compiler_params=grant(20),
            cost_estimate=cost(0.06 * share + 0.3),
            name="inverse",
        )(my_waves[first : first + share], joined, table, *after)

    def values(first, share, parts, base):
        def body(near_ref, far_ref, *refs):
            start = refs[lon_count][...] if base else None
            refs[-1][...] = zonal_values(
                lon_count, share, first, near_ref, far_ref, refs[:lon_count], start
            )

        return pl.pallas_call(
            body,
            out_shape=like((grid_count, lon_dev), F32),
            in_specs=[VMEM] * (2 + lon_count + len(base)),
            out_specs=VMEM,
            compiler_params=grant(24),
            cost_estimate=cost(0.025 * share),
            name="values",
        )(near, far, *parts, *base)

    base, first, coefs = [], slots_dev, []
    for chunk in reversed(range(len(CUTS))):
        share = CUTS[chunk]
        first -= share
        own, sent = inverse(first, share, coefs)
        coefs = [sent]
        parts = from_owners(own, sent)
        base = [values(first, share, parts, base)]
    spectrum = spectrum.reshape(2, levels, degree_dev, slots_dev).transpose(2, 3, 0, 1)
    return (base[0].reshape(level_fields.shape), spectrum)


def shards(
    level_fields, wind_field, zonal_step, quad_weight, legendre, wave_table, damping, vertical
):
    levels, _, rows_half, lon_dev = level_fields.shape
    slots_dev, _, columns = legendre.shape
    lat_count = lax.axis_size("lat")
    lon_count = lax.axis_size("lon")
    degree_dev = columns // lat_count
    body = tiled
    if (
        rows_half % 16
        or degree_dev % 16
        or lon_dev % LANES
        or slots_dev != sum(CUTS)
        or levels != 2
        or lat_count & (lat_count - 1)
        or lat_count < 4
        or lon_count & (lon_count - 1)
        or lon_count != 4
    ):
        body = untiled
    return body(
        level_fields,
        wind_field,
        zonal_step,
        quad_weight,
        legendre,
        wave_table,
        damping,
        vertical,
    )


def solution(mesh):
    return jax.shard_map(
        shards,
        mesh=mesh,
        in_specs=(
            P(None, None, "lat", "lon"),
            P(None, None, "lat", "lon"),
            P("lat"),
            P("lat"),
            P("lon", "lat", None),
            P(),
            P(),
            P(),
        ),
        out_specs=(P(None, None, "lat", "lon"), P("lat", "lon", None, None)),
        check_vma=False,
    )
```

```python
import math

import jax
import jax.numpy as jnp
from jax import lax
from jax.experimental import pallas as pl
from jax.experimental.pallas import tpu as pltpu
from jax.sharding import PartitionSpec as P


NLON = 2560
M = 640


HIGHEST_PRECISION = lax.Precision.HIGHEST


def padded(cells, sides, width):
    for axis, dim in sides:
        count = lax.axis_size(axis)
        head = lax.slice_in_dim(cells, 0, width, axis=dim)
        tail = lax.slice_in_dim(cells, cells.shape[dim] - width, cells.shape[dim], axis=dim)
        cells = jnp.concatenate(
            [
                lax.ppermute(tail, axis, [(i, (i + 1) % count) for i in range(count)]),
                cells,
                lax.ppermute(head, axis, [((i + 1) % count, i) for i in range(count)]),
            ],
            axis=dim,
        )
    return cells


def angle_table(waves, columns):
    return (waves[:, None] * columns[None, :] % NLON).astype(jnp.float32) * (2.0 * math.pi / NLON)


def correct(spectrum, degrees, damping, vertical):
    modal = jnp.einsum("kl,nmcl->nmck", vertical, spectrum, precision=HIGHEST_PRECISION)
    divisor = 1.0 + damping[None, :] * (degrees * (degrees + 1)).astype(jnp.float32)[
        :, None
    ] / float(M * M)
    modal = modal / divisor[:, None, None, :]
    return jnp.einsum("kl,nmck->nmcl", vertical, modal, precision=HIGHEST_PRECISION)


def untiled(
    level_fields, wind_field, zonal_step, quad_weight, legendre, wave_table, damping, vertical
):
    levels, hemis, rows_half, lon_dev = level_fields.shape
    slots_dev = legendre.shape[0]
    lat_count = lax.axis_size("lat")
    lat_index = lax.axis_index("lat")
    lon_index = lax.axis_index("lon")
    degree_dev = M // lat_count
    grid_count = levels * hemis * rows_half
    contract_last = (((1,), (1,)), ((), ()))
    contract_first = (((0,), (0,)), ((), ()))
    batch_slots = (((2,), (1,)), ((0,), (0,)))
    extended = padded(level_fields, (("lat", 2), ("lon", 3)), 1)
    eastward = extended[:, :, 1:-1, 2:]
    westward = extended[:, :, 1:-1, :-2]
    toward = extended[:, :, 2:, 1:-1]
    poleward = extended[:, :, :-2, 1:-1]
    row_number = jnp.arange(rows_half)
    at_equator = (row_number == rows_half - 1) & (lat_index == lat_count - 1)
    toward = jnp.where(at_equator[:, None], level_fields[:, ::-1, -1:, :], toward)
    at_pole = (row_number == 0) & (lat_index == 0)
    poleward = jnp.where(at_pole[:, None], 0.0, poleward)
    tendency = wind_field[0] * zonal_step[:, None] * (eastward - westward) + 0.25 * wind_field[
        1
    ] * (toward - poleward)
    stepped = level_fields - tendency
    my_waves = lax.dynamic_slice_in_dim(wave_table, lon_index * slots_dev, slots_dev)
    portion = lax.all_gather(stepped, "lon", axis=3, tiled=True)
    lon_width = portion.shape[3]
    columns = jnp.arange(lon_width, dtype=jnp.int32)
    angles = angle_table(my_waves, columns)
    values = portion.reshape(grid_count, lon_width)
    cosine_sum = lax.dot_general(
        jnp.cos(angles), values, contract_last, precision=HIGHEST_PRECISION
    )
    sine_sum = lax.dot_general(jnp.sin(angles), values, contract_last, precision=HIGHEST_PRECISION)
    cosine_sum, sine_sum = (cosine_sum, sine_sum)
    fourier = jnp.stack([cosine_sum, -sine_sum], axis=1) / math.sqrt(NLON)
    weighted = (fourier.reshape(slots_dev, 2, levels, hemis, rows_half) * quad_weight).astype(
        jnp.bfloat16
    )
    weighted = weighted.reshape(slots_dev, 2 * levels * hemis, rows_half)
    table_part = legendre
    summed = lax.dot_general(weighted, table_part, batch_slots, preferred_element_type=jnp.float32)
    summed = summed.reshape(slots_dev, 2, levels, hemis, degree_dev * lax.axis_size("lat"))
    degrees = jnp.arange(degree_dev * lax.axis_size("lat"), dtype=jnp.int32)
    parity = jnp.where((degrees[None, :] - my_waves[:, None]) % 2 == 0, 1.0, -1.0)
    kept_mask = degrees[None, :] >= my_waves[:, None]
    combined = summed[:, :, :, 0] + parity[:, None, None, :] * summed[:, :, :, 1]
    combined = jnp.where(kept_mask[:, None, None, :], combined, 0.0)
    raw = lax.psum_scatter(combined.transpose(3, 0, 1, 2), "lat", scatter_dimension=0, tiled=True)
    my_degrees = lat_index * degree_dev + jnp.arange(degree_dev, dtype=jnp.int32)
    spectrum = correct(raw, my_degrees, damping, vertical)
    portion = lax.all_gather(spectrum.astype(jnp.bfloat16), "lat", axis=0, tiled=True)
    row_count = portion.shape[0]
    table_part = legendre
    degrees = jnp.arange(row_count, dtype=jnp.int32)
    even_mask = ((degrees[None, :] - my_waves[:, None]) % 2 == 0)[:, :, None]
    arranged = portion.transpose(1, 0, 2, 3).reshape(slots_dev, row_count, 2 * levels)
    even_sum = lax.dot_general(
        table_part,
        jnp.where(even_mask, arranged, 0),
        batch_slots,
        preferred_element_type=jnp.float32,
    )
    odd_sum = lax.dot_general(
        table_part,
        jnp.where(even_mask, 0, arranged),
        batch_slots,
        preferred_element_type=jnp.float32,
    )
    even_sum, odd_sum = (even_sum, odd_sum)
    coefs = jnp.stack([even_sum + odd_sum, even_sum - odd_sum], axis=1) / math.sqrt(M)
    coefs = (
        coefs.reshape(slots_dev, 2, rows_half, 2, levels)
        .transpose(0, 3, 4, 1, 2)
        .reshape(slots_dev, 2, grid_count)
    )
    my_columns = lon_index * lon_dev + jnp.arange(lon_dev, dtype=jnp.int32)
    portion = lax.all_gather(coefs, "lon", axis=0, tiled=True)
    factor = jnp.where(wave_table == 0, 1.0, 2.0)[:, None]
    angles = angle_table(wave_table, my_columns)
    totals = lax.dot_general(
        portion[:, 0], jnp.cos(angles) * factor, contract_first, precision=HIGHEST_PRECISION
    )
    grid_out = totals - lax.dot_general(
        portion[:, 1], jnp.sin(angles) * factor, contract_first, precision=HIGHEST_PRECISION
    )
    new_fields = (grid_out / math.sqrt(NLON)).reshape(level_fields.shape)
    return (new_fields, spectrum)


CUTS = (64, 64, 32)
GROUP = 16
LANES = 128
F32 = jnp.float32
BF16 = jnp.bfloat16


def split_halves(value):
    high = value.astype(BF16)
    return high, (value - high.astype(F32)).astype(BF16)


def dot_rows(left, right):
    return lax.dot_general(left, right, (((1,), (1,)), ((), ())), preferred_element_type=F32)


def dot_columns(left, right):
    return lax.dot_general(left, right, (((0,), (0,)), ((), ())), preferred_element_type=F32)


def pairs(count, step):
    return [(i, i ^ step) for i in range(count)]


def load_kernel(fields_hbm, winds_hbm, fields_ref, winds_ref, *refs):
    first_row, last_row, first_column, last_column, semaphores = refs
    fields_copy = pltpu.make_async_copy(fields_hbm, fields_ref, semaphores.at[0])
    winds_copy = pltpu.make_async_copy(winds_hbm, winds_ref, semaphores.at[1])
    fields_copy.start()
    winds_copy.start()
    fields_copy.wait()
    count, rows, columns = fields_ref.shape
    for p in range(count):
        first_row[p : p + 1, :] = fields_ref[p, 0:1, :]
        last_row[p : p + 1, :] = fields_ref[p, rows - 1 : rows, :]
        first_column[:, p : p + 1] = fields_ref[p, :, 0:1]
        last_column[:, p : p + 1] = fields_ref[p, :, columns - 1 : columns]
    winds_copy.wait()


def load_table_kernel(after_ref, table_hbm, table_ref, semaphores):
    parts = semaphores.shape[0]
    share = table_ref.shape[0] // parts
    copies = [
        pltpu.make_async_copy(
            table_hbm.at[pl.ds(i * share, share)],
            table_ref.at[pl.ds(i * share, share)],
            semaphores.at[i],
        )
        for i in range(parts)
    ]
    for copy in copies:
        copy.start()
    for copy in copies:
        copy.wait()


def advance(flags, fields_ref, wind_ref, step_ref, above, below, before, after, stepped_ref):
    count, rows, columns = fields_ref.shape
    lane = lax.broadcasted_iota(jnp.int32, (rows, columns), 1)
    row = lax.broadcasted_iota(jnp.int32, (rows, columns), 0)
    square = (rows, rows)
    diagonal = lax.broadcasted_iota(jnp.int32, square, 0) == lax.broadcasted_iota(
        jnp.int32, square, 1
    )
    steps = jnp.sum(jnp.where(diagonal, step_ref[...], 0.0), axis=1, keepdims=True)
    for p in range(count):
        h = p % 2
        field = fields_ref[p]
        eastward = jnp.where(
            lane == columns - 1, after[:, p : p + 1], pltpu.roll(field, columns - 1, 1)
        )
        westward = jnp.where(lane == 0, before[:, p : p + 1], pltpu.roll(field, 1, 1))
        other = fields_ref[p ^ 1, rows - 1 : rows, :]
        low_edge = jnp.where(flags[1] == 1, other, below[p : p + 1, :])
        high_edge = jnp.where(flags[0] == 1, 0.0, above[p : p + 1, :])
        toward = jnp.where(row == rows - 1, low_edge, pltpu.roll(field, rows - 1, 0))
        poleward = jnp.where(row == 0, high_edge, pltpu.roll(field, 1, 0))
        tendency = wind_ref[h] * steps * (eastward - westward) + 0.25 * wind_ref[
            2 + h
        ] * (toward - poleward)
        stepped_ref[p * rows : (p + 1) * rows, :] = field - tendency


def table_rows(near, far, first, share, blocks, part):
    per_block = near.shape[0] // blocks
    half = far.shape[1] // 2
    out = []
    for k in range(blocks):
        at = pl.ds(k * per_block + first, share)
        near_cos, near_sin = near[at, :LANES], near[at, LANES:]
        far_cos, far_sin = far[at, :half], far[at, half:]
        columns = []
        for j in range(half):
            c, s = far_cos[:, j : j + 1], far_sin[:, j : j + 1]
            if part:
                columns.append(-(s * near_cos + c * near_sin))
            else:
                columns.append(c * near_cos - s * near_sin)
        out.append(jnp.concatenate(columns, axis=1))
    return jnp.concatenate(out, axis=0)


def zonal_sums(blocks, share, first, stepped_ref, near, far, outs):
    high, low = split_halves(stepped_ref[...])
    count = stepped_ref.shape[0]
    for part in range(2):
        rows_high, rows_low = split_halves(table_rows(near, far, first, share, blocks, part))
        sums = dot_rows(rows_high, high) + (dot_rows(rows_high, low) + dot_rows(rows_low, high))
        lanes = slice(part * count, (part + 1) * count)
        own, pair = outs
        for k in range(0, blocks, 2):
            own[k // 2, :, lanes] = sums[k * share : (k + 1) * share, :]
            pair[k // 2, :, lanes] = sums[(k + 1) * share : (k + 2) * share, :].astype(BF16)


def forward_kernel(
    blocks, sections, rows, degree_dev, first, last, waves_ref, place_ref, *refs
):
    received = refs[:blocks]
    weight_ref, table_ref = refs[blocks : blocks + 2]
    rest = refs[blocks + 2 :]
    spread_ref, kept_ref, turned_ref = rest[-3:]
    step = pl.program_id(0)
    half = sections // 2
    levels = half // 2
    group = GROUP
    columns = table_ref.shape[2]
    share = spread_ref.shape[0]

    @pl.when(step == 0)
    def _():
        total = received[0][...].astype(F32)
        for other in received[1:]:
            total = total + other[...].astype(F32)
        total = total * weight_ref[...]
        for c in range(2):
            for level in range(levels):
                for h in range(2):
                    at = ((c * levels + level) * 2 + h) * rows
                    spread_ref[:, h * half + level * 2 + c, 0:rows] = total[:, at : at + rows]

    degree = lax.broadcasted_iota(jnp.int32, (2 * half, columns), 1)
    row = lax.broadcasted_iota(jnp.int32, (2 * half, 1), 0)
    for u in range(0, group, 2):
        sums = []
        for v in (u, u + 1):
            high, low = split_halves(spread_ref[step * group + v, :, 0:rows])
            both = jnp.concatenate([high.astype(F32), low.astype(F32)], axis=0).astype(BF16)
            total = jnp.dot(both, table_ref[first + step * group + v], preferred_element_type=F32)
            sums.append(total[:sections] + total[sections:])
        north = jnp.concatenate([sums[0][:half], sums[1][:half]], axis=0)
        south = jnp.concatenate([sums[0][half:], sums[1][half:]], axis=0)
        slot = step * group + u
        past = degree - jnp.where(row < half, waves_ref[slot], waves_ref[slot + 1])
        combined = north + jnp.where(past & 1 == 0, south, -south)
        combined = jnp.where(past >= 0, combined, 0.0)
        at = pl.ds(pl.multiple_of(slot * half, 2 * half), 2 * half)
        for t in range(columns // LANES):
            kept_ref[t, at, :] = combined[:, t * LANES : (t + 1) * LANES]

    @pl.when(step == pl.num_programs(0) - 1)
    def _():
        target = turned_ref if last else rest[-4]
        for t in range(columns // LANES):
            tile = jnp.concatenate(
                [kept_ref[t, pl.ds(j, share, stride=half), :] for j in range(half)], axis=0
            )
            target[t * LANES : (t + 1) * LANES, :] = tile.T
        if not last:
            return
        earlier, (own_ref, other_ref) = rest[:-5], rest[-5:-3]
        for j in range(own_ref.shape[0]):
            for out, k in ((own_ref, 2 * j), (other_ref, 2 * j + 1)):
                at = pl.ds(pl.multiple_of((place_ref[0] ^ k) * degree_dev, 8), degree_dev)
                done = 0
                for source in (*earlier, turned_ref):
                    wide = source.shape[1]
                    out[j, :, done : done + wide] = source[at, :]
                    done += wide


def correct_kernel(
    cuts, levels, place_ref, damping_ref, vertical_ref, sum_ref, *refs
):
    others, (rounded_ref, spectrum_ref) = refs[:-2], refs[-2:]
    total = sum_ref[...]
    for other in others:
        total = total + other[...].astype(F32)
    count = total.shape[0]
    degree = place_ref[0] * count + lax.broadcasted_iota(jnp.int32, (count, 1), 0)
    growth = (degree * (degree + 1)).astype(F32) / float(M * M)
    scale = [1.0 / (1.0 + damping_ref[k] * growth) for k in range(levels)]
    at, slot = 0, 0
    for share in cuts:
        wide = 2 * share
        raw = [total[:, at + l * wide : at + (l + 1) * wide] for l in range(levels)]
        modal = [
            sum(vertical_ref[k, l] * raw[l] for l in range(levels)) * scale[k]
            for k in range(levels)
        ]
        for l in range(levels):
            value = sum(vertical_ref[k, l] * modal[k] for k in range(levels))
            rounded_ref[:, at + l * wide : at + (l + 1) * wide] = value.astype(BF16)
            for c in range(2):
                spectrum_ref[c * levels + l, :, slot : slot + share] = value[
                    :, c * share : (c + 1) * share
                ]
        at, slot = at + levels * wide, slot + share


def inverse_kernel(sections, rows, first, waves_ref, joined_ref, table_ref, *refs):
    own_ref, out_ref, kept_ref, spread_ref = refs
    step = pl.program_id(0)
    half = sections // 2
    levels = half // 2
    group = GROUP
    columns = table_ref.shape[2]
    share = spread_ref.shape[0]

    @pl.when(step == 0)
    def _():
        for t in range(columns // LANES):
            tile = joined_ref[t * LANES : (t + 1) * LANES, half * first : half * (first + share)]
            turned = tile.astype(F32).T
            for j in range(half):
                kept_ref[t, pl.ds(j, share, stride=half), :] = turned[
                    j * share : (j + 1) * share, :
                ]

    degree = lax.broadcasted_iota(jnp.int32, (2 * half, columns), 1)
    row = lax.broadcasted_iota(jnp.int32, (2 * half, 1), 0)
    upper = row < half
    for u in range(0, group, 2):
        slot = step * group + u
        at = pl.ds(pl.multiple_of(slot * half, 2 * half), 2 * half)
        values = jnp.concatenate(
            [kept_ref[t, at, :] for t in range(columns // LANES)], axis=1
        )
        even = (degree - jnp.where(upper, waves_ref[slot], waves_ref[slot + 1])) & 1 == 0
        evens = jnp.where(even, values, 0.0)
        odds = pltpu.roll(jnp.where(even, 0.0, values), half, 0)
        for v in range(2):
            both = jnp.where(upper, odds, evens) if v else jnp.where(upper, evens, odds)
            sums = dot_rows(both.astype(BF16), table_ref[first + slot + v])
            factor = jnp.where(waves_ref[slot + v] == 0, 1.0, 2.0) / math.sqrt(M)
            sums = sums * factor
            swapped = pltpu.roll(sums, half, 0)
            less = sums - swapped if v else swapped - sums
            spread_ref[slot + v, :, 0:rows] = jnp.where(upper, sums + swapped, less)

    @pl.when(step == pl.num_programs(0) - 1)
    def _():
        for c in range(2):
            for level in range(levels):
                for h in range(2):
                    at = ((c * levels + level) * 2 + h) * rows
                    value = spread_ref[:, h * half + level * 2 + c, 0:rows]
                    own_ref[:, at : at + rows] = value
                    out_ref[:, at : at + rows] = value.astype(out_ref.dtype)


def zonal_values(blocks, share, first, near, far, received, total):
    for part in range(2):
        count = received[0].shape[1] // 2
        rows_high, rows_low = split_halves(table_rows(near, far, first, share, blocks, part))
        lanes = slice(part * count, (part + 1) * count)
        own_high, own_low = split_halves(received[0][:, lanes])
        coefs = jnp.concatenate([own_high] + [other[:, lanes] for other in received[1:]], axis=0)
        term = dot_columns(coefs, rows_high) + dot_columns(coefs, rows_low)
        term = term + dot_columns(own_low, rows_high[:share])
        total = term if total is None else total + term
    return total


VMEM = pl.BlockSpec(memory_space=pltpu.VMEM)
SMEM = pl.BlockSpec(memory_space=pltpu.SMEM)
HBM = pl.BlockSpec(memory_space=pltpu.HBM)


def grant(size):
    return pltpu.CompilerParams(vmem_limit_bytes=size << 20)


def cost(microseconds):
    return pl.CostEstimate(flops=0, bytes_accessed=int(microseconds * 3.3e6), transcendentals=0)


def like(shape, dtype):
    return jax.ShapeDtypeStruct(shape, dtype)


def whole_block(shape):
    return pl.BlockSpec(shape, lambda *_: (0,) * len(shape))


def tiled(
    level_fields, wind_field, zonal_step, quad_weight, legendre, wave_table, damping, vertical
):
    levels, hemis, rows_half, lon_dev = level_fields.shape
    slots_dev, _, columns = legendre.shape
    lat_count = lax.axis_size("lat")
    lon_count = lax.axis_size("lon")
    degree_dev = columns // lat_count
    lat_index = lax.axis_index("lat")
    lon_index = lax.axis_index("lon")
    planes = levels * hemis
    grid_count = planes * rows_half
    sections = 2 * planes
    half = sections // 2
    width = 2 * grid_count
    fields = level_fields.reshape(planes, rows_half, lon_dev)
    winds = wind_field.reshape(2 * hemis, rows_half, lon_dev)

    fields, winds, first_row, last_row, first_column, last_column = pl.pallas_call(
        load_kernel,
        out_shape=[pltpu.VMEM(fields.shape, F32), pltpu.VMEM(winds.shape, F32)]
        + [like((planes, lon_dev), F32)] * 2
        + [like((rows_half, planes), F32)] * 2,
        in_specs=[HBM] * 2,
        out_specs=[VMEM] * 6,
        scratch_shapes=[pltpu.SemaphoreType.DMA((2,))],
        compiler_params=grant(8),
        cost_estimate=cost(1.5),
        name="load",
    )(*[pltpu.with_memory_space_constraint(value, pltpu.HBM) for value in (fields, winds)])
    up = [(i, (i + 1) % lat_count) for i in range(lat_count)]
    east = [(i, (i + 1) % lon_count) for i in range(lon_count)]
    down = [(j, i) for i, j in up]
    west = [(j, i) for i, j in east]
    above = lax.ppermute(last_row, "lat", up)
    below = lax.ppermute(first_row, "lat", down)
    before = lax.ppermute(last_column, "lon", east)
    after = lax.ppermute(first_column, "lon", west)

    order = [
        lax.dynamic_slice_in_dim(wave_table, (lon_index ^ k) * slots_dev, slots_dev)
        for k in range(lon_count)
    ]
    my_waves = order[0]
    waves = jnp.concatenate(order)
    near_angle = angle_table(waves, jnp.arange(LANES, dtype=jnp.int32))
    near = jnp.concatenate([jnp.cos(near_angle), jnp.sin(near_angle)], axis=1)
    far_angle = angle_table(
        waves, lon_index * lon_dev + LANES * jnp.arange(lon_dev // LANES, dtype=jnp.int32)
    )
    far = jnp.concatenate([jnp.cos(far_angle), jnp.sin(far_angle)], axis=1) / math.sqrt(NLON)

    flags = jnp.stack([lat_index == 0, lat_index == lat_count - 1]).astype(jnp.int32)
    place = lat_index.astype(jnp.int32).reshape(1)
    weight_row = jnp.tile(quad_weight, sections)[None, :]

    def sums_shape(share):
        return [like((lon_count // 2, share, width), dtype) for dtype in (F32, BF16)]

    def first_sums(flags_ref, fields_ref, winds_ref, step_ref, *refs):
        edges, near_ref, far_ref, stepped_ref = refs[:4], *refs[4:7]
        advance(flags_ref, fields_ref, winds_ref, step_ref, *edges, stepped_ref)
        zonal_sums(lon_count, CUTS[0], 0, stepped_ref, near_ref, far_ref, refs[7:])

    stepped, *pieces = pl.pallas_call(
        first_sums,
        out_shape=[like((grid_count, lon_dev), F32)] + sums_shape(CUTS[0]),
        in_specs=[SMEM] + [VMEM] * 9,
        out_specs=[VMEM] * 3,
        compiler_params=grant(20),
        cost_estimate=cost(3.0),
        name="advance_and_sums",
    )(
        flags, fields, winds, zonal_step[None, :], above, below, before, after, near, far
    )

    def later_sums(chunk, first, after):
        share = CUTS[chunk]

        def body(stepped_ref, near_ref, far_ref, after_ref, *outs):
            zonal_sums(lon_count, share, first, stepped_ref, near_ref, far_ref, outs)

        return pl.pallas_call(
            body,
            out_shape=sums_shape(share),
            in_specs=[VMEM] * 4,
            out_specs=[VMEM] * 2,
            compiler_params=grant(20),
            cost_estimate=cost(0.035 * share),
            name="sums",
        )(stepped, near, far, after)

    def swap(value, axis, step):
        return lax.ppermute(value, axis, pairs(lax.axis_size(axis), step))

    def to_owners(own, pair):
        pair = swap(pair, "lon", 1)
        parts = [own[0], pair[0]]
        for k in range(1, lon_count // 2):
            joint = (own[k] + pair[k].astype(F32)).astype(BF16)
            parts.append(swap(joint, "lon", 2 * k))
        return parts

    def from_owners(own, coefs):
        parts = [own, swap(coefs, "lon", 1)]
        for k in range(1, lon_count // 2):
            distant = swap(coefs, "lon", 2 * k)
            parts += [distant, swap(distant, "lon", 1)]
        return parts

    swapped, first = [to_owners(*pieces)], CUTS[0]
    for chunk in range(1, len(CUTS)):
        pieces = later_sums(chunk, first, pieces[0])
        swapped.append(to_owners(*pieces))
        first += CUTS[chunk]
    table = pl.pallas_call(
        load_table_kernel,
        out_shape=pltpu.VMEM(legendre.shape, BF16),
        in_specs=[VMEM, HBM],
        out_specs=VMEM,
        scratch_shapes=[pltpu.SemaphoreType.DMA((4,))],
        compiler_params=grant(8),
        cost_estimate=cost(5.7),
        name="load_table",
    )(pieces[0], pltpu.with_memory_space_constraint(legendre, pltpu.HBM))


    def forward(first, share, parts, earlier, last):
        if last:
            shape = (lat_count // 2, degree_dev, half * slots_dev)
            shapes = [like(shape, F32)] * 2
        else:
            shapes = [like((columns, half * share), F32)]
        return pl.pallas_call(
            lambda *refs: forward_kernel(
                len(parts), sections, rows_half, degree_dev, first, last, *refs
            ),
            out_shape=shapes,
            grid_spec=pltpu.PrefetchScalarGridSpec(
                num_scalar_prefetch=2,
                grid=(share // GROUP,),
                in_specs=[whole_block((share, width))] * len(parts)
                + [whole_block((1, width)), VMEM]
                + [whole_block(other.shape) for other in earlier],
                out_specs=[whole_block(shape.shape) for shape in shapes],
                scratch_shapes=[
                    pltpu.VMEM((share, sections, LANES), F32),
                    pltpu.VMEM((columns // LANES, half * share, LANES), F32),
                    pltpu.VMEM((columns, half * share), F32),
                ],
            ),
            compiler_params=grant(20),
            cost_estimate=cost(0.05 * share + 0.7),
            name="forward",
        )(my_waves[first : first + share], place, *parts, weight_row, table, *earlier)

    earlier, first = [], 0
    for chunk, share in enumerate(CUTS):
        last = chunk == len(CUTS) - 1
        earlier += forward(first, share, swapped[chunk], earlier, last)
        first += share
    own, other = earlier[-2:]

    other = swap(other, "lat", 1)
    sums = [own[j] + other[j] for j in range(lat_count // 2)]
    sums = [sums[0]] + [swap(sums[j].astype(BF16), "lat", 2 * j) for j in range(1, lat_count // 2)]
    rounded, spectrum = pl.pallas_call(
        lambda *refs: correct_kernel(CUTS, levels, *refs),
        out_shape=[
            like((degree_dev, half * slots_dev), BF16),
            like((half, degree_dev, slots_dev), F32),
        ],
        in_specs=[SMEM] * 3 + [VMEM] * len(sums),
        out_specs=[VMEM] * 2,
        compiler_params=grant(8),
        name="correct",
    )(place, damping, vertical, *sums)
    joined = lax.all_gather(rounded, "lat", axis=0, tiled=True)

    def inverse(first, share, after):
        count = 3 + len(after)
        return pl.pallas_call(
            lambda *refs: inverse_kernel(sections, rows_half, first, *refs[:3], *refs[count:]),
            out_shape=[like((share, width), F32), like((share, width), BF16)],
            grid_spec=pltpu.PrefetchScalarGridSpec(
                num_scalar_prefetch=1,
                grid=(share // GROUP,),
                in_specs=[whole_block(joined.shape), VMEM] + [VMEM] * len(after),
                out_specs=[whole_block((share, width))] * 2,
                scratch_shapes=[
                    pltpu.VMEM((columns // LANES, half * share, LANES), F32),
                    pltpu.VMEM((share, sections, LANES), F32),
                ],
            ),
            compiler_params=grant(20),
            cost_estimate=cost(0.06 * share + 0.3),
            name="inverse",
        )(my_waves[first : first + share], joined, table, *after)

    def values(first, share, parts, base):
        def body(near_ref, far_ref, *refs):
            start = refs[lon_count][...] if base else None
            refs[-1][...] = zonal_values(
                lon_count, share, first, near_ref, far_ref, refs[:lon_count], start
            )

        return pl.pallas_call(
            body,
            out_shape=like((grid_count, lon_dev), F32),
            in_specs=[VMEM] * (2 + lon_count + len(base)),
            out_specs=VMEM,
            compiler_params=grant(24),
            cost_estimate=cost(0.025 * share),
            name="values",
        )(near, far, *parts, *base)

    base, first, coefs = [], slots_dev, []
    for chunk in reversed(range(len(CUTS))):
        share = CUTS[chunk]
        first -= share
        own, sent = inverse(first, share, coefs)
        coefs = [sent]
        parts = from_owners(own, sent)
        base = [values(first, share, parts, base)]
    spectrum = spectrum.reshape(2, levels, degree_dev, slots_dev).transpose(2, 3, 0, 1)
    return (base[0].reshape(level_fields.shape), spectrum)


def shards(
    level_fields, wind_field, zonal_step, quad_weight, legendre, wave_table, damping, vertical
):
    levels, _, rows_half, lon_dev = level_fields.shape
    slots_dev, _, columns = legendre.shape
    lat_count = lax.axis_size("lat")
    lon_count = lax.axis_size("lon")
    degree_dev = columns // lat_count
    body = tiled
    if (
        rows_half % 16
        or degree_dev % 16
        or lon_dev % LANES
        or slots_dev != sum(CUTS)
        or levels != 2
        or lat_count & (lat_count - 1)
        or lat_count < 4
        or lon_count & (lon_count - 1)
        or lon_count != 4
    ):
        body = untiled
    return body(
        level_fields,
        wind_field,
        zonal_step,
        quad_weight,
        legendre,
        wave_table,
        damping,
        vertical,
    )


def solution(mesh):
    return jax.shard_map(
        shards,
        mesh=mesh,
        in_specs=(
            P(None, None, "lat", "lon"),
            P(None, None, "lat", "lon"),
            P("lat"),
            P("lat"),
            P("lon", "lat", None),
            P(),
            P(),
            P(),
        ),
        out_specs=(P(None, None, "lat", "lon"), P("lat", "lon", None, None)),
        check_vma=False,
    )
```

```python
import math

import jax
import jax.numpy as jnp
import numpy as np
from jax import lax
from jax.experimental import pallas as pl
from jax.experimental.pallas import tpu as pltpu
from jax.sharding import PartitionSpec as P


NLON = 2560
M = 640


HIGHEST_PRECISION = lax.Precision.HIGHEST


def padded(cells, sides, width):
    for axis, dim in sides:
        count = lax.axis_size(axis)
        head = lax.slice_in_dim(cells, 0, width, axis=dim)
        tail = lax.slice_in_dim(cells, cells.shape[dim] - width, cells.shape[dim], axis=dim)
        cells = jnp.concatenate(
            [
                lax.ppermute(tail, axis, [(i, (i + 1) % count) for i in range(count)]),
                cells,
                lax.ppermute(head, axis, [((i + 1) % count, i) for i in range(count)]),
            ],
            axis=dim,
        )
    return cells


def angle_table(waves, columns):
    return (waves[:, None] * columns[None, :] % NLON).astype(jnp.float32) * (2.0 * math.pi / NLON)


def correct(spectrum, degrees, damping, vertical):
    modal = jnp.einsum("kl,nmcl->nmck", vertical, spectrum, precision=HIGHEST_PRECISION)
    divisor = 1.0 + damping[None, :] * (degrees * (degrees + 1)).astype(jnp.float32)[
        :, None
    ] / float(M * M)
    modal = modal / divisor[:, None, None, :]
    return jnp.einsum("kl,nmck->nmcl", vertical, modal, precision=HIGHEST_PRECISION)


def untiled(
    level_fields, wind_field, zonal_step, quad_weight, legendre, wave_table, damping, vertical
):
    levels, hemis, rows_half, lon_dev = level_fields.shape
    slots_dev = legendre.shape[0]
    lat_count = lax.axis_size("lat")
    lat_index = lax.axis_index("lat")
    lon_index = lax.axis_index("lon")
    degree_dev = M // lat_count
    grid_count = levels * hemis * rows_half
    contract_last = (((1,), (1,)), ((), ()))
    contract_first = (((0,), (0,)), ((), ()))
    batch_slots = (((2,), (1,)), ((0,), (0,)))
    extended = padded(level_fields, (("lat", 2), ("lon", 3)), 1)
    eastward = extended[:, :, 1:-1, 2:]
    westward = extended[:, :, 1:-1, :-2]
    toward = extended[:, :, 2:, 1:-1]
    poleward = extended[:, :, :-2, 1:-1]
    row_number = jnp.arange(rows_half)
    at_equator = (row_number == rows_half - 1) & (lat_index == lat_count - 1)
    toward = jnp.where(at_equator[:, None], level_fields[:, ::-1, -1:, :], toward)
    at_pole = (row_number == 0) & (lat_index == 0)
    poleward = jnp.where(at_pole[:, None], 0.0, poleward)
    tendency = wind_field[0] * zonal_step[:, None] * (eastward - westward) + 0.25 * wind_field[
        1
    ] * (toward - poleward)
    stepped = level_fields - tendency
    my_waves = lax.dynamic_slice_in_dim(wave_table, lon_index * slots_dev, slots_dev)
    portion = lax.all_gather(stepped, "lon", axis=3, tiled=True)
    lon_width = portion.shape[3]
    columns = jnp.arange(lon_width, dtype=jnp.int32)
    angles = angle_table(my_waves, columns)
    values = portion.reshape(grid_count, lon_width)
    cosine_sum = lax.dot_general(
        jnp.cos(angles), values, contract_last, precision=HIGHEST_PRECISION
    )
    sine_sum = lax.dot_general(jnp.sin(angles), values, contract_last, precision=HIGHEST_PRECISION)
    cosine_sum, sine_sum = (cosine_sum, sine_sum)
    fourier = jnp.stack([cosine_sum, -sine_sum], axis=1) / math.sqrt(NLON)
    weighted = (fourier.reshape(slots_dev, 2, levels, hemis, rows_half) * quad_weight).astype(
        jnp.bfloat16
    )
    weighted = weighted.reshape(slots_dev, 2 * levels * hemis, rows_half)
    table_part = legendre
    summed = lax.dot_general(weighted, table_part, batch_slots, preferred_element_type=jnp.float32)
    summed = summed.reshape(slots_dev, 2, levels, hemis, degree_dev * lax.axis_size("lat"))
    degrees = jnp.arange(degree_dev * lax.axis_size("lat"), dtype=jnp.int32)
    parity = jnp.where((degrees[None, :] - my_waves[:, None]) % 2 == 0, 1.0, -1.0)
    kept_mask = degrees[None, :] >= my_waves[:, None]
    combined = summed[:, :, :, 0] + parity[:, None, None, :] * summed[:, :, :, 1]
    combined = jnp.where(kept_mask[:, None, None, :], combined, 0.0)
    raw = lax.psum_scatter(combined.transpose(3, 0, 1, 2), "lat", scatter_dimension=0, tiled=True)
    my_degrees = lat_index * degree_dev + jnp.arange(degree_dev, dtype=jnp.int32)
    spectrum = correct(raw, my_degrees, damping, vertical)
    portion = lax.all_gather(spectrum.astype(jnp.bfloat16), "lat", axis=0, tiled=True)
    row_count = portion.shape[0]
    table_part = legendre
    degrees = jnp.arange(row_count, dtype=jnp.int32)
    even_mask = ((degrees[None, :] - my_waves[:, None]) % 2 == 0)[:, :, None]
    arranged = portion.transpose(1, 0, 2, 3).reshape(slots_dev, row_count, 2 * levels)
    even_sum = lax.dot_general(
        table_part,
        jnp.where(even_mask, arranged, 0),
        batch_slots,
        preferred_element_type=jnp.float32,
    )
    odd_sum = lax.dot_general(
        table_part,
        jnp.where(even_mask, 0, arranged),
        batch_slots,
        preferred_element_type=jnp.float32,
    )
    even_sum, odd_sum = (even_sum, odd_sum)
    coefs = jnp.stack([even_sum + odd_sum, even_sum - odd_sum], axis=1) / math.sqrt(M)
    coefs = (
        coefs.reshape(slots_dev, 2, rows_half, 2, levels)
        .transpose(0, 3, 4, 1, 2)
        .reshape(slots_dev, 2, grid_count)
    )
    my_columns = lon_index * lon_dev + jnp.arange(lon_dev, dtype=jnp.int32)
    portion = lax.all_gather(coefs, "lon", axis=0, tiled=True)
    factor = jnp.where(wave_table == 0, 1.0, 2.0)[:, None]
    angles = angle_table(wave_table, my_columns)
    totals = lax.dot_general(
        portion[:, 0], jnp.cos(angles) * factor, contract_first, precision=HIGHEST_PRECISION
    )
    grid_out = totals - lax.dot_general(
        portion[:, 1], jnp.sin(angles) * factor, contract_first, precision=HIGHEST_PRECISION
    )
    new_fields = (grid_out / math.sqrt(NLON)).reshape(level_fields.shape)
    return (new_fields, spectrum)


CUTS = (64, 64, 32)
GROUP = 16
LANES = 128
F32 = jnp.float32
BF16 = jnp.bfloat16


def split_halves(value):
    high = value.astype(BF16)
    return high, (value - high.astype(F32)).astype(BF16)


def dot_rows(left, right):
    return lax.dot_general(left, right, (((1,), (1,)), ((), ())), preferred_element_type=F32)


def dot_columns(left, right):
    return lax.dot_general(left, right, (((0,), (0,)), ((), ())), preferred_element_type=F32)


def pairs(count, step):
    return [(i, i ^ step) for i in range(count)]


def load_kernel(count_in, *refs):
    sources, targets = refs[:count_in], refs[count_in : 2 * count_in]
    first_row, last_row, first_column, last_column, semaphores = refs[2 * count_in :]
    copies = [
        pltpu.make_async_copy(source, target, semaphores.at[i])
        for i, (source, target) in enumerate(zip(sources, targets))
    ]
    for copy in copies:
        copy.start()
    copies[0].wait()
    fields_ref = targets[0]
    count, rows, columns = fields_ref.shape
    for p in range(count):
        first_row[p : p + 1, :] = fields_ref[p, 0:1, :]
        last_row[p : p + 1, :] = fields_ref[p, rows - 1 : rows, :]
        first_column[:, p : p + 1] = fields_ref[p, :, 0:1]
        last_column[:, p : p + 1] = fields_ref[p, :, columns - 1 : columns]
    for copy in copies[1:]:
        copy.wait()


def advance(place, lat_count, fields_ref, wind_ref, step_ref, above, below, before, after, stepped_ref):
    count, rows, columns = fields_ref.shape
    lane = lax.broadcasted_iota(jnp.int32, (rows, columns), 1)
    row = lax.broadcasted_iota(jnp.int32, (rows, columns), 0)
    square = (rows, rows)
    diagonal = lax.broadcasted_iota(jnp.int32, square, 0) == lax.broadcasted_iota(
        jnp.int32, square, 1
    )
    steps = jnp.sum(jnp.where(diagonal, step_ref[...], 0.0), axis=1, keepdims=True)
    for p in range(count):
        h = p % 2
        field = fields_ref[p]
        eastward = jnp.where(
            lane == columns - 1, after[:, p : p + 1], pltpu.roll(field, columns - 1, 1)
        )
        westward = jnp.where(lane == 0, before[:, p : p + 1], pltpu.roll(field, 1, 1))
        other = fields_ref[p ^ 1, rows - 1 : rows, :]
        low_edge = jnp.where(place[0] == lat_count - 1, other, below[p : p + 1, :])
        high_edge = jnp.where(place[0] == 0, 0.0, above[p : p + 1, :])
        toward = jnp.where(row == rows - 1, low_edge, pltpu.roll(field, rows - 1, 0))
        poleward = jnp.where(row == 0, high_edge, pltpu.roll(field, 1, 0))
        tendency = wind_ref[h] * steps * (eastward - westward) + 0.25 * wind_ref[
            2 + h
        ] * (toward - poleward)
        stepped_ref[p * rows : (p + 1) * rows, :] = field - tendency


def table_rows(place, turns, first, share, blocks, part):
    per_block = turns.shape[0] // blocks
    half = (turns.shape[1] - 2 * LANES) // 2
    out = []
    for k in range(blocks):
        at = pl.ds(pl.multiple_of((place[1] ^ k) * per_block + first, 32), share)
        near_cos, near_sin = turns[at, :LANES], turns[at, LANES : 2 * LANES]
        far = turns[at, 2 * LANES :]
        columns = []
        for j in range(half):
            c, s = far[:, j : j + 1], far[:, half + j : half + j + 1]
            if part:
                columns.append(-(s * near_cos + c * near_sin))
            else:
                columns.append(c * near_cos - s * near_sin)
        out.append(jnp.concatenate(columns, axis=1))
    return jnp.concatenate(out, axis=0)


def zonal_sums(place, blocks, share, first, stepped_ref, turns, outs):
    high, low = split_halves(stepped_ref[...])
    count = stepped_ref.shape[0]
    for part in range(2):
        rows_high, rows_low = split_halves(table_rows(place, turns, first, share, blocks, part))
        sums = dot_rows(rows_high, high) + (dot_rows(rows_high, low) + dot_rows(rows_low, high))
        lanes = slice(part * count, (part + 1) * count)
        own, pair = outs
        for k in range(0, blocks, 2):
            own[k // 2, :, lanes] = sums[k * share : (k + 1) * share, :]
            pair[k // 2, :, lanes] = sums[(k + 1) * share : (k + 2) * share, :].astype(BF16)


def forward_kernel(
    blocks, sections, rows, degree_dev, base, first, last, waves_ref, place_ref, *refs
):
    received = refs[:blocks]
    weight_ref, table_ref = refs[blocks : blocks + 2]
    rest = refs[blocks + 2 :]
    copies = []
    if not first:
        table_hbm, *rest, table_ref, s0, s1, s2, semaphores = table_ref, *rest
        rest = [*rest, s0, s1, s2]
        copies = [
            pltpu.make_async_copy(
                table_hbm.at[pl.ds(i * GROUP, GROUP)],
                table_ref.at[pl.ds(i * GROUP, GROUP)],
                semaphores.at[i],
            )
            for i in range(semaphores.shape[0])
        ]
    spread_ref, kept_ref, turned_ref = rest[-3:]
    step = pl.program_id(0)
    half = sections // 2
    levels = half // 2
    group = GROUP
    columns = table_ref.shape[2]
    share = spread_ref.shape[0]

    @pl.when(step == 0)
    def _():
        for copy in copies:
            copy.start()
        total = received[0][...].astype(F32)
        for other in received[1:]:
            total = total + other[...].astype(F32)
        for c in range(2):
            for level in range(levels):
                for h in range(2):
                    at = ((c * levels + level) * 2 + h) * rows
                    spread_ref[:, h * half + level * 2 + c, 0:rows] = (
                        total[:, at : at + rows] * weight_ref[...]
                    )

    for i, copy in enumerate(copies[: share // group]):
        pl.when(step == i)(copy.wait)
    degree = lax.broadcasted_iota(jnp.int32, (2 * half, columns), 1)
    row = lax.broadcasted_iota(jnp.int32, (2 * half, 1), 0)
    mine = place_ref[1] * base + first
    for u in range(0, group, 2):
        sums = []
        for v in (u, u + 1):
            high, low = split_halves(spread_ref[step * group + v, :, 0:rows])
            both = jnp.concatenate([high.astype(F32), low.astype(F32)], axis=0).astype(BF16)
            total = jnp.dot(both, table_ref[first + step * group + v], preferred_element_type=F32)
            sums.append(total[:sections] + total[sections:])
        north = jnp.concatenate([sums[0][:half], sums[1][:half]], axis=0)
        south = jnp.concatenate([sums[0][half:], sums[1][half:]], axis=0)
        slot = step * group + u
        past = degree - jnp.where(
            row < half, waves_ref[mine + slot], waves_ref[mine + slot + 1]
        )
        combined = north + jnp.where(past & 1 == 0, south, -south)
        combined = jnp.where(past >= 0, combined, 0.0)
        at = pl.ds(pl.multiple_of(slot * half, 2 * half), 2 * half)
        for t in range(columns // LANES):
            kept_ref[t, at, :] = combined[:, t * LANES : (t + 1) * LANES]

    @pl.when(step == pl.num_programs(0) - 1)
    def _():
        for copy in copies[share // group :]:
            copy.wait()
        target = turned_ref if last else rest[-4]
        for t in range(columns // LANES):
            tile = jnp.concatenate(
                [kept_ref[t, pl.ds(j, share, stride=half), :] for j in range(half)], axis=0
            )
            target[t * LANES : (t + 1) * LANES, :] = tile.T
        if not last:
            return
        earlier, (own_ref, other_ref) = rest[:-5], rest[-5:-3]
        for j in range(own_ref.shape[0]):
            for out, k in ((own_ref, 2 * j), (other_ref, 2 * j + 1)):
                at = pl.ds(pl.multiple_of((place_ref[0] ^ k) * degree_dev, 8), degree_dev)
                done = 0
                for source in (*earlier, turned_ref):
                    wide = source.shape[1]
                    out[j, :, done : done + wide] = source[at, :]
                    done += wide


def correct_kernel(
    cuts, levels, place_ref, damping_ref, vertical_ref, sum_ref, *refs
):
    others, (rounded_ref, spectrum_ref) = refs[:-2], refs[-2:]
    total = sum_ref[...]
    for other in others:
        total = total + other[...].astype(F32)
    count = total.shape[0]
    degree = place_ref[0] * count + lax.broadcasted_iota(jnp.int32, (count, 1), 0)
    growth = (degree * (degree + 1)).astype(F32) / float(M * M)
    scale = [1.0 / (1.0 + damping_ref[k] * growth) for k in range(levels)]
    at, slot = 0, 0
    for share in cuts:
        wide = 2 * share
        raw = [total[:, at + l * wide : at + (l + 1) * wide] for l in range(levels)]
        modal = [
            sum(vertical_ref[k, l] * raw[l] for l in range(levels)) * scale[k]
            for k in range(levels)
        ]
        for l in range(levels):
            value = sum(vertical_ref[k, l] * modal[k] for k in range(levels))
            rounded_ref[:, at + l * wide : at + (l + 1) * wide] = value.astype(BF16)
            for c in range(2):
                spectrum_ref[c * levels + l, :, slot : slot + share] = value[
                    :, c * share : (c + 1) * share
                ]
        at, slot = at + levels * wide, slot + share


def inverse_kernel(sections, rows, base, first, waves_ref, place_ref, joined_ref, table_ref, *refs):
    own_ref, out_ref, kept_ref, spread_ref = refs
    step = pl.program_id(0)
    half = sections // 2
    levels = half // 2
    group = GROUP
    columns = table_ref.shape[2]
    share = spread_ref.shape[0]

    @pl.when(step == 0)
    def _():
        for t in range(columns // LANES):
            tile = joined_ref[t * LANES : (t + 1) * LANES, half * first : half * (first + share)]
            turned = tile.astype(F32).T
            for j in range(half):
                kept_ref[t, pl.ds(j, share, stride=half), :] = turned[
                    j * share : (j + 1) * share, :
                ]

    degree = lax.broadcasted_iota(jnp.int32, (2 * half, columns), 1)
    row = lax.broadcasted_iota(jnp.int32, (2 * half, 1), 0)
    upper = row < half
    mine = place_ref[1] * base + first
    for u in range(0, group, 2):
        slot = step * group + u
        at = pl.ds(pl.multiple_of(slot * half, 2 * half), 2 * half)
        values = jnp.concatenate(
            [kept_ref[t, at, :] for t in range(columns // LANES)], axis=1
        )
        even = (degree - jnp.where(upper, waves_ref[mine + slot], waves_ref[mine + slot + 1])) & 1 == 0
        evens = jnp.where(even, values, 0.0)
        odds = pltpu.roll(jnp.where(even, 0.0, values), half, 0)
        for v in range(2):
            both = jnp.where(upper, odds, evens) if v else jnp.where(upper, evens, odds)
            sums = dot_rows(both.astype(BF16), table_ref[first + slot + v])
            factor = jnp.where(waves_ref[mine + slot + v] == 0, 1.0, 2.0) / math.sqrt(M)
            sums = sums * factor
            swapped = pltpu.roll(sums, half, 0)
            less = sums - swapped if v else swapped - sums
            spread_ref[slot + v, :, 0:rows] = jnp.where(upper, sums + swapped, less)

    @pl.when(step == pl.num_programs(0) - 1)
    def _():
        for c in range(2):
            for level in range(levels):
                for h in range(2):
                    at = ((c * levels + level) * 2 + h) * rows
                    value = spread_ref[:, h * half + level * 2 + c, 0:rows]
                    own_ref[:, at : at + rows] = value
                    out_ref[:, at : at + rows] = value.astype(out_ref.dtype)


def zonal_values(place, blocks, share, first, turns, received, total):
    for part in range(2):
        count = received[0].shape[1] // 2
        rows_high, rows_low = split_halves(table_rows(place, turns, first, share, blocks, part))
        lanes = slice(part * count, (part + 1) * count)
        own_high, own_low = split_halves(received[0][:, lanes])
        coefs = jnp.concatenate([own_high] + [other[:, lanes] for other in received[1:]], axis=0)
        term = dot_columns(coefs, rows_high) + dot_columns(coefs, rows_low)
        term = term + dot_columns(own_low, rows_high[:share])
        total = term if total is None else total + term
    return total


VMEM = pl.BlockSpec(memory_space=pltpu.VMEM)
SMEM = pl.BlockSpec(memory_space=pltpu.SMEM)
HBM = pl.BlockSpec(memory_space=pltpu.HBM)


def grant(size):
    return pltpu.CompilerParams(vmem_limit_bytes=size << 20)


def cost(microseconds):
    return pl.CostEstimate(flops=0, bytes_accessed=int(microseconds * 3.3e6), transcendentals=0)


def like(shape, dtype):
    return jax.ShapeDtypeStruct(shape, dtype)


def whole_block(shape):
    return pl.BlockSpec(shape, lambda *_: (0,) * len(shape))


def tiled(
    level_fields, wind_field, zonal_step, quad_weight, legendre, wave_table, damping, vertical
):
    levels, hemis, rows_half, lon_dev = level_fields.shape
    slots_dev, _, columns = legendre.shape
    lat_count = lax.axis_size("lat")
    lon_count = lax.axis_size("lon")
    degree_dev = columns // lat_count
    lat_index = lax.axis_index("lat")
    lon_index = lax.axis_index("lon")
    planes = levels * hemis
    grid_count = planes * rows_half
    sections = 2 * planes
    half = sections // 2
    width = 2 * grid_count
    fields = level_fields.reshape(planes, rows_half, lon_dev)
    winds = wind_field.reshape(2 * hemis, rows_half, lon_dev)

    arrays = [fields, winds, zonal_step[None, :], quad_weight[None, :]]
    fields, winds, step_row, weight_row, first_row, last_row, first_column, last_column = (
        pl.pallas_call(
            lambda *refs: load_kernel(len(arrays), *refs),
            out_shape=[pltpu.VMEM(value.shape, F32) for value in arrays]
            + [like((planes, lon_dev), F32)] * 2
            + [like((rows_half, planes), F32)] * 2,
            in_specs=[HBM] * len(arrays),
            out_specs=[VMEM] * (4 + len(arrays)),
            scratch_shapes=[pltpu.SemaphoreType.DMA((len(arrays),))],
            compiler_params=grant(8),
            cost_estimate=cost(1.5),
            name="load",
        )(*[pltpu.with_memory_space_constraint(value, pltpu.HBM) for value in arrays])
    )
    up = [(i, (i + 1) % lat_count) for i in range(lat_count)]
    east = [(i, (i + 1) % lon_count) for i in range(lon_count)]
    down = [(j, i) for i, j in up]
    west = [(j, i) for i, j in east]
    above = lax.ppermute(last_row, "lat", up)
    below = lax.ppermute(first_row, "lat", down)
    before = lax.ppermute(last_column, "lon", east)
    after = lax.ppermute(first_column, "lon", west)

    tiles = lon_dev // LANES
    tile_columns = lon_index * lon_dev + LANES * jnp.arange(tiles, dtype=jnp.int32)
    near_columns = jnp.arange(LANES, dtype=jnp.int32)
    at_columns = jnp.concatenate([near_columns, near_columns, tile_columns, tile_columns])
    ahead = np.repeat([NLON // 4, 0, NLON // 4, 0], [LANES, LANES, tiles, tiles]).astype(np.int32)
    scale = np.repeat([1.0, 1.0 / math.sqrt(NLON)], [2 * LANES, 2 * tiles]).astype(np.float32)
    turned = (wave_table[:, None] * at_columns[None, :] + ahead[None, :]) % NLON
    turns = jnp.sin(turned.astype(F32) * (2.0 * math.pi / NLON)) * scale[None, :]
    place = jnp.stack([lat_index, lon_index]).astype(jnp.int32)
    waves = pltpu.with_memory_space_constraint(wave_table, pltpu.HBM)

    def sums_shape(share):
        return [like((lon_count // 2, share, width), dtype) for dtype in (F32, BF16)]

    def first_sums(place_ref, fields_ref, winds_ref, step_ref, *refs):
        edges, turns_ref, stepped_ref = refs[:4], refs[4], refs[5]
        advance(place_ref, lat_count, fields_ref, winds_ref, step_ref, *edges, stepped_ref)
        zonal_sums(place_ref, lon_count, CUTS[0], 0, stepped_ref, turns_ref, refs[6:])

    stepped, *pieces = pl.pallas_call(
        first_sums,
        out_shape=[like((grid_count, lon_dev), F32)] + sums_shape(CUTS[0]),
        in_specs=[SMEM] + [VMEM] * 8,
        out_specs=[VMEM] * 3,
        compiler_params=grant(20),
        cost_estimate=cost(3.0),
        name="advance_and_sums",
    )(place, fields, winds, step_row, above, below, before, after, turns)

    def later_sums(chunk, first, after):
        share = CUTS[chunk]

        def body(place_ref, stepped_ref, turns_ref, after_ref, *outs):
            zonal_sums(place_ref, lon_count, share, first, stepped_ref, turns_ref, outs)

        return pl.pallas_call(
            body,
            out_shape=sums_shape(share),
            in_specs=[SMEM] + [VMEM] * 3,
            out_specs=[VMEM] * 2,
            compiler_params=grant(20),
            cost_estimate=cost(0.035 * share),
            name="sums",
        )(place, stepped, turns, after)

    def swap(value, axis, step):
        return lax.ppermute(value, axis, pairs(lax.axis_size(axis), step))

    def to_owners(own, pair):
        pair = swap(pair, "lon", 1)
        parts = [own[0], pair[0]]
        for k in range(1, lon_count // 2):
            joint = (own[k] + pair[k].astype(F32)).astype(BF16)
            parts.append(swap(joint, "lon", 2 * k))
        return parts

    def from_owners(own, coefs):
        parts = [own, swap(coefs, "lon", 1)]
        for k in range(1, lon_count // 2):
            distant = swap(coefs, "lon", 2 * k)
            parts += [distant, swap(distant, "lon", 1)]
        return parts

    swapped, first = [to_owners(*pieces)], CUTS[0]
    for chunk in range(1, len(CUTS)):
        pieces = later_sums(chunk, first, pieces[0])
        swapped.append(to_owners(*pieces))
        first += CUTS[chunk]

    def forward(first, share, parts, table, earlier, last):
        if last:
            shape = (lat_count // 2, degree_dev, half * slots_dev)
            shapes = [like(shape, F32)] * 2
        else:
            shapes = [like((columns, half * share), F32)]
        specs = [whole_block(shape.shape) for shape in shapes]
        loads, table_spec = [], VMEM
        if not first:
            shapes = shapes + [pltpu.VMEM(legendre.shape, BF16)]
            specs = specs + [VMEM]
            loads, table_spec = [pltpu.SemaphoreType.DMA((slots_dev // GROUP,))], HBM
        return pl.pallas_call(
            lambda *refs: forward_kernel(
                len(parts), sections, rows_half, degree_dev, slots_dev, first, last, *refs
            ),
            out_shape=shapes,
            grid_spec=pltpu.PrefetchScalarGridSpec(
                num_scalar_prefetch=2,
                grid=(share // GROUP,),
                in_specs=[whole_block((share, width))] * len(parts)
                + [whole_block((1, rows_half)), table_spec]
                + [whole_block(other.shape) for other in earlier],
                out_specs=specs,
                scratch_shapes=[
                    pltpu.VMEM((share, sections, LANES), F32),
                    pltpu.VMEM((columns // LANES, half * share, LANES), F32),
                    pltpu.VMEM((columns, half * share), F32),
                ]
                + loads,
            ),
            compiler_params=grant(20),
            cost_estimate=cost(0.05 * share + 0.7),
            name="forward",
        )(waves, place, *parts, weight_row, table, *earlier)

    table = pltpu.with_memory_space_constraint(legendre, pltpu.HBM)
    earlier, first = [], 0
    for chunk, share in enumerate(CUTS):
        last = chunk == len(CUTS) - 1
        outs = forward(first, share, swapped[chunk], table, earlier, last)
        if not first:
            *outs, table = outs
        earlier += outs
        first += share
    own, other = earlier[-2:]

    other = swap(other, "lat", 1)
    sums = [own[j] + other[j] for j in range(lat_count // 2)]
    sums = [sums[0]] + [swap(sums[j].astype(BF16), "lat", 2 * j) for j in range(1, lat_count // 2)]
    rounded, spectrum = pl.pallas_call(
        lambda *refs: correct_kernel(CUTS, levels, *refs),
        out_shape=[
            like((degree_dev, half * slots_dev), BF16),
            like((half, degree_dev, slots_dev), F32),
        ],
        in_specs=[SMEM] * 3 + [VMEM] * len(sums),
        out_specs=[VMEM] * 2,
        compiler_params=grant(8),
        name="correct",
    )(place, damping, vertical, *sums)
    joined = lax.all_gather(rounded, "lat", axis=0, tiled=True)

    def inverse(first, share, after):
        count = 4 + len(after)
        return pl.pallas_call(
            lambda *refs: inverse_kernel(
                sections, rows_half, slots_dev, first, *refs[:4], *refs[count:]
            ),
            out_shape=[like((share, width), F32), like((share, width), BF16)],
            grid_spec=pltpu.PrefetchScalarGridSpec(
                num_scalar_prefetch=2,
                grid=(share // GROUP,),
                in_specs=[whole_block(joined.shape), VMEM] + [VMEM] * len(after),
                out_specs=[whole_block((share, width))] * 2,
                scratch_shapes=[
                    pltpu.VMEM((columns // LANES, half * share, LANES), F32),
                    pltpu.VMEM((share, sections, LANES), F32),
                ],
            ),
            compiler_params=grant(20),
            cost_estimate=cost(0.06 * share + 0.3),
            name="inverse",
        )(waves, place, joined, table, *after)

    def values(first, share, parts, base):
        def body(place_ref, turns_ref, *refs):
            start = refs[lon_count][...] if base else None
            refs[-1][...] = zonal_values(
                place_ref, lon_count, share, first, turns_ref, refs[:lon_count], start
            )

        return pl.pallas_call(
            body,
            out_shape=like((grid_count, lon_dev), F32),
            in_specs=[SMEM] + [VMEM] * (1 + lon_count + len(base)),
            out_specs=VMEM,
            compiler_params=grant(24),
            cost_estimate=cost(0.025 * share),
            name="values",
        )(place, turns, *parts, *base)

    base, first, coefs = [], slots_dev, []
    for chunk in reversed(range(len(CUTS))):
        share = CUTS[chunk]
        first -= share
        own, sent = inverse(first, share, coefs)
        coefs = [sent]
        parts = from_owners(own, sent)
        base = [values(first, share, parts, base)]
    spectrum = spectrum.reshape(2, levels, degree_dev, slots_dev).transpose(2, 3, 0, 1)
    return (base[0].reshape(level_fields.shape), spectrum)


def shards(
    level_fields, wind_field, zonal_step, quad_weight, legendre, wave_table, damping, vertical
):
    levels, _, rows_half, lon_dev = level_fields.shape
    slots_dev, _, columns = legendre.shape
    lat_count = lax.axis_size("lat")
    lon_count = lax.axis_size("lon")
    degree_dev = columns // lat_count
    body = tiled
    if (
        rows_half % 16
        or degree_dev % 16
        or lon_dev % LANES
        or slots_dev != sum(CUTS)
        or levels != 2
        or lat_count & (lat_count - 1)
        or lat_count < 4
        or lon_count & (lon_count - 1)
        or lon_count != 4
    ):
        body = untiled
    return body(
        level_fields,
        wind_field,
        zonal_step,
        quad_weight,
        legendre,
        wave_table,
        damping,
        vertical,
    )


def solution(mesh):
    return jax.shard_map(
        shards,
        mesh=mesh,
        in_specs=(
            P(None, None, "lat", "lon"),
            P(None, None, "lat", "lon"),
            P("lat"),
            P("lat"),
            P("lon", "lat", None),
            P(),
            P(),
            P(),
        ),
        out_specs=(P(None, None, "lat", "lon"), P("lat", "lon", None, None)),
        check_vma=False,
    )
```
